512 devices in a mesh: rot: 32 (over y, x_hi, core), tag: 16 (over z, x_lo).
Axes of the slice: x: 4 (x_hi: 2, x_lo: 2; x = x_hi * 2 + x_lo), y: 8, z: 8, core: 2. Of those that a mesh axis runs over, the one named last changes fastest.
Arguments:
- user_factors: bfloat16 [262144, 512], P(('rot', 'tag')), may hold values from -1.1953125 to 1.1953125
- item_factors: bfloat16 [32768, 512], P('rot'), may hold values from -1.1953125 to 1.1953125
- tag_factors: bfloat16 [8192, 512], P('tag'), may hold values from -1.1953125 to 1.1953125
- rating_tiles: int32 [8192, 2], P(('rot', 'tag')), may hold values from 0 to 7, as said below
- rating_counts: int32 [512], P(('rot', 'tag')), may hold values from 1 to 16, as said below
- ratings: bfloat16 [8192, 128, 128], P(('rot', 'tag')), may hold values from -6 to 6
- tag_tiles: int32 [8192, 2], P(('rot', 'tag')), may hold values from 0 to 7, as said below
- tag_values: bfloat16 [8192, 128, 128], P(('rot', 'tag')), may hold values from -6 to 6
Outputs:
- new_users: bfloat16 [262144, 512], P(('rot', 'tag'))
- rotated_items: bfloat16 [32768, 512], P('rot')
- new_tags: bfloat16 [8192, 512], P('tag')
The draws below stay inside these ranges and needn't reach their ends.
Inputs may be any that keep to these rules, and one draw needn't show every extreme that they name: `rating_tiles`: each device's 16 slots hold distinct tiles; column 0 is below 4, column 1 below 8. `rating_counts`: uneven over devices; some device has all 16 slots live. `tag_tiles`: each device has exactly 16 distinct tiles; column 0 is below 8, column 1 below 4.
All inputs are finite; a program needn't handle non-finite values.
Results may differ from the reference program's by a relative error of at most 0.0043.
Values may be sent and summed in bfloat16 or wider, within the bound.
No kernel may reach another device: no remote copies, remote signals or barrier semaphores. Data moves between devices by JAX's collectives and lax.ppermute only.
A program may use at most 64 MiB of HBM per device.

```python
import jax
import jax.numpy as jnp
from jax import lax

R = 512
TILE = 128
UB = 512
IB = 1024
TAG_DEV = 512
RSLOTS = 16
XSLOTS = 16
DEVICES_ALL = 512
USERS = 262144
ITEMS = 32768
TAGS = 8192
N_ROT = 32
N_TAG = 16


def tile_coords(key, rows_tiles, cols_tiles, slots):
    keys = jax.random.split(key, N_ROT * N_TAG)

    def one_device(device_key):
        order = jax.random.permutation(device_key, rows_tiles * cols_tiles)[:slots]
        return jnp.stack([order // cols_tiles, order % cols_tiles], axis=1)
    return jax.vmap(one_device)(keys).reshape(N_ROT * N_TAG * slots, 2).astype(jnp.int32)


def draw_rating_tiles(key, part):
    return tile_coords(jax.random.fold_in(key, 11), UB // TILE, IB // TILE, RSLOTS)


def draw_tag_tiles(key, part):
    return tile_coords(jax.random.fold_in(key, 23), IB // TILE, TAG_DEV // TILE, XSLOTS)


def draw_rating_counts(key, part):
    first_key, second_key = jax.random.split(jax.random.fold_in(key, 37))
    counts = jax.random.randint(first_key, (N_ROT * N_TAG,), 1, RSLOTS + 1)
    fullest = jax.random.randint(second_key, (), 0, N_ROT * N_TAG)
    return counts.at[fullest].set(RSLOTS).astype(jnp.int32)


def block_scale(own_key, dims, shards, smallest, largest):
    level, own = 1.0, jax.random.fold_in(own_key, 6)
    for axis_at, blocks in shards:
        draws = jnp.exp(jax.random.uniform(jax.random.fold_in(own, axis_at), (blocks,), jnp.float32, smallest / len(shards), largest / len(shards)))
        level = level * jnp.repeat(draws, dims[axis_at] // blocks).reshape([-1 if axis == axis_at else 1 for axis in range(len(dims))])
    return level


def noise(own_key, dims, scale, bound, shards=(), kind=jnp.bfloat16):
    factor_of = block_scale(own_key, dims, shards, -0.22, 0.18) if shards else 1.0
    values = jax.random.normal(own_key, dims, jnp.float32) * scale * factor_of
    return jnp.minimum(jnp.maximum(values, -bound), bound).astype(kind)


def setup_inputs(seed: int = 0) -> dict:
    key_list = jax.random.split(jax.random.key(seed), 9)
    user_factors = noise(key_list[0], (USERS, R), 0.2, 1.1953125, ((0, 512),))
    item_factors = noise(key_list[1], (ITEMS, R), 0.2, 1.1953125, ((0, 32),))
    tag_factors = noise(key_list[2], (TAGS, R), 0.2, 1.1953125, ((0, 16),))
    rating_tiles = draw_rating_tiles(jax.random.fold_in(key_list[8], 71), 0)
    rating_counts = draw_rating_counts(jax.random.fold_in(key_list[8], 71), 0)
    ratings = noise(key_list[5], (DEVICES_ALL * RSLOTS, TILE, TILE), 1.0, 6.0, ((0, 512),))
    tag_tiles = draw_tag_tiles(jax.random.fold_in(key_list[8], 71), 0)
    tag_values = noise(key_list[7], (DEVICES_ALL * XSLOTS, TILE, TILE), 1.0, 6.0, ((0, 512),))
    return {"user_factors": user_factors, "item_factors": item_factors, "tag_factors": tag_factors, "rating_tiles": rating_tiles, "rating_counts": rating_counts, "ratings": ratings, "tag_tiles": tag_tiles, "tag_values": tag_values}


def reference(user_factors, item_factors, tag_factors, rating_tiles, rating_counts, ratings, tag_tiles, tag_values):
    devices_all = N_ROT * N_TAG
    ublocks = user_factors.reshape(devices_all, UB // TILE, TILE, R)
    vblocks = item_factors.reshape(N_ROT, IB // TILE, TILE, R)
    wblocks = tag_factors.reshape(N_TAG, TAG_DEV // TILE, TILE, R)
    rcoords = rating_tiles.reshape(devices_all, RSLOTS, 2)
    rvalues = ratings.reshape(devices_all, RSLOTS, TILE, TILE)
    xcoords = tag_tiles.reshape(devices_all, XSLOTS, 2)
    xvalues = tag_values.reshape(devices_all, XSLOTS, TILE, TILE)

    def one_device(carry, device):
        item_sum, tag_sum = carry
        rot_index = device // N_TAG
        tag_index = device % N_TAG
        ublock = ublocks[device].astype(jnp.float32)
        vblock = vblocks[rot_index].astype(jnp.float32)
        wblock = wblocks[tag_index].astype(jnp.float32)
        coords = rcoords[device]
        user_tiles = ublock[coords[:, 0]]
        item_tiles = vblock[coords[:, 1]]
        predicted = jnp.einsum('sur,sir->sui', user_tiles, item_tiles)
        live = (jnp.arange(RSLOTS) < rating_counts[device])[:, None, None]
        rating_err = jnp.where(live, predicted - rvalues[device].astype(jnp.float32), 0.0)
        rating_err = rating_err.astype(jnp.bfloat16).astype(jnp.float32)
        user_part = jnp.einsum('sui,sir->sur', rating_err, item_tiles)
        item_part = jnp.einsum('sui,sur->sir', rating_err, user_tiles)
        tcoords = xcoords[device]
        item_rows = vblock[tcoords[:, 0]]
        tag_rows = wblock[tcoords[:, 1]]
        tag_err = jnp.einsum('sir,sjr->sij', item_rows, tag_rows) - xvalues[device].astype(jnp.float32)
        tag_err = tag_err.astype(jnp.bfloat16).astype(jnp.float32)
        item_from_tags = jnp.einsum('sij,sjr->sir', tag_err, tag_rows)
        tag_part = jnp.einsum('sij,sir->sjr', tag_err, item_rows)
        user_grad = jnp.zeros((UB // TILE, TILE, R), jnp.float32).at[coords[:, 0]].add(user_part)
        item_grad = jnp.zeros((IB // TILE, TILE, R), jnp.float32).at[coords[:, 1]].add(item_part)
        item_grad = item_grad.at[tcoords[:, 0]].add(item_from_tags)
        tag_grad = jnp.zeros((TAG_DEV // TILE, TILE, R), jnp.float32).at[tcoords[:, 1]].add(tag_part)
        item_sum = item_sum.at[rot_index].add(item_grad)
        tag_sum = tag_sum.at[tag_index].add(tag_grad)
        new_block = (ublock - 0.04 * (user_grad + 0.05 * ublock)).astype(jnp.bfloat16)
        return (item_sum, tag_sum), new_block

    start = (jnp.zeros((N_ROT, IB // TILE, TILE, R), jnp.float32), jnp.zeros((N_TAG, TAG_DEV // TILE, TILE, R), jnp.float32))
    (item_sum, tag_sum), new_blocks = lax.scan(one_device, start, jnp.arange(devices_all).astype(jnp.int32))
    new_users = new_blocks.reshape(USERS, R)
    items32 = item_factors.astype(jnp.float32)
    new_items = (items32 - 0.04 * (item_sum.reshape(ITEMS, R) + 0.05 * items32)).astype(jnp.bfloat16)
    rotated_items = jnp.roll(new_items.reshape(N_ROT, IB, R), 1, axis=0).reshape(ITEMS, R)
    tags32 = tag_factors.astype(jnp.float32)
    new_tags = (tags32 - 0.04 * (tag_sum.reshape(TAGS, R) + 0.05 * tags32)).astype(jnp.bfloat16)
    return (new_users, rotated_items, new_tags)
```

```python
import jax
import jax.numpy as jnp
from jax import lax
from jax.experimental import pallas as pl
from jax.experimental.pallas import tpu as pltpu
from jax.sharding import PartitionSpec as P

TILE = 128
F32 = jnp.float32
BF16 = jnp.bfloat16


def tile(index):
    return pl.ds(pl.multiple_of(index * TILE, TILE), TILE)


def dot_rows(left, right):
    return lax.dot_general(left, right, (((1,), (1,)), ((), ())), preferred_element_type=F32)


def grads_kernel(
    rt_ref, rc_ref, xt_ref, u_ref, v_ref, w_ref, r_ref, x_ref,
    item_ref, tag_ref, err_ref, err_t, tag_err, tag_err_t,
):
    err_ref[...] = jnp.zeros_like(err_ref)
    err_t[...] = jnp.zeros_like(err_t)
    tag_err[...] = jnp.zeros_like(tag_err)
    tag_err_t[...] = jnp.zeros_like(tag_err_t)
    count = rc_ref[0]
    for s in range(r_ref.shape[0]):
        a, c = tile(rt_ref[0, s]), tile(rt_ref[1, s])
        e = dot_rows(u_ref[a, :], v_ref[c, :]) - r_ref[s].astype(F32)
        e = jnp.where(s < count, e, 0.0)
        err_ref[a, c] = e.astype(BF16)
        err_t[c, a] = e.T.astype(BF16)
    for s in range(x_ref.shape[0]):
        a, c = tile(xt_ref[0, s]), tile(xt_ref[1, s])
        e = dot_rows(v_ref[a, :], w_ref[c, :]) - x_ref[s].astype(F32)
        tag_err[a, c] = e.astype(BF16)
        tag_err_t[c, a] = e.T.astype(BF16)
    step = 256
    for i in range(0, item_ref.shape[0], step):
        rows = pl.ds(i, step)
        part = jnp.dot(err_t[rows, :], u_ref[...], preferred_element_type=F32)
        part += jnp.dot(tag_err[rows, :], w_ref[...], preferred_element_type=F32)
        item_ref[rows, :] = part.astype(BF16)
    for i in range(0, tag_ref.shape[0], step):
        rows = pl.ds(i, step)
        part = jnp.dot(tag_err_t[rows, :], v_ref[...], preferred_element_type=F32)
        tag_ref[rows, :] = part.astype(BF16)


def users_kernel(err_ref, u_ref, v_ref, out_ref):
    step = 256
    for i in range(0, out_ref.shape[0], step):
        rows = pl.ds(i, step)
        grad = jnp.dot(err_ref[rows, :], v_ref[...], preferred_element_type=F32)
        old = u_ref[rows, :].astype(F32)
        out_ref[rows, :] = (old - 0.04 * (grad + 0.05 * old)).astype(BF16)


def whole():
    return pl.BlockSpec(memory_space=pltpu.VMEM)


def scalars():
    return pl.BlockSpec(memory_space=pltpu.SMEM)


def partials(rt, rc, xt, u, v, w, r, x):
    users, rank = u.shape
    items, tags = v.shape[0], w.shape[0]
    return pl.pallas_call(
        grads_kernel,
        out_shape=(
            jax.ShapeDtypeStruct((items, rank), BF16),
            jax.ShapeDtypeStruct((tags, rank), BF16),
            jax.ShapeDtypeStruct((users, items), BF16),
        ),
        in_specs=[scalars()] * 3 + [whole()] * 5,
        out_specs=(whole(),) * 3,
        scratch_shapes=[
            pltpu.VMEM((items, users), BF16),
            pltpu.VMEM((items, tags), BF16),
            pltpu.VMEM((tags, items), BF16),
        ],
        compiler_params=pltpu.CompilerParams(vmem_limit_bytes=24 << 20),
        cost_estimate=pl.CostEstimate(flops=3 << 30, bytes_accessed=6 << 20, transcendentals=0),
    )(rt, rc, xt, u, v, w, r, x)


def updated_users(err, u, v):
    return pl.pallas_call(
        users_kernel,
        out_shape=jax.ShapeDtypeStruct(u.shape, BF16),
        in_specs=[whole()] * 3,
        out_specs=whole(),
        compiler_params=pltpu.CompilerParams(vmem_limit_bytes=16 << 20),
        cost_estimate=pl.CostEstimate(flops=1 << 30, bytes_accessed=4 << 20, transcendentals=0),
    )(err, u, v)


def exchanged(pieces, axis):
    return lax.all_to_all(pieces, axis, 0, 0)


def stepped(old, pieces):
    total = jnp.sum(pieces.astype(F32), axis=0)
    old = old.astype(F32)
    return (old - 0.04 * (total + 0.05 * old)).astype(BF16)


def shard_of(block, axis):
    n = lax.axis_size(axis)
    size = block.shape[0] // n
    return lax.dynamic_slice_in_dim(block, lax.axis_index(axis) * size, size, 0)


def gathered(shard, axis):
    n = lax.axis_size(axis)
    copies = jnp.broadcast_to(shard, (n,) + shard.shape)
    return exchanged(copies, axis).reshape(n * shard.shape[0], shard.shape[1])


def on_device(u, v, w, rating_tiles, rating_counts, ratings, tag_tiles, tag_values):
    rank = u.shape[1]
    n_rot, n_tag = lax.axis_size("rot"), lax.axis_size("tag")
    item_part, tag_part, err = partials(
        rating_tiles.T, rating_counts, tag_tiles.T, u, v, w, ratings, tag_values
    )
    item_pieces = exchanged(item_part.reshape(n_tag, -1, rank), "tag")
    tag_pieces = exchanged(tag_part.reshape(n_rot, -1, rank), "rot")
    new_users = updated_users(err, u, v)
    item_shard = stepped(shard_of(v, "tag"), item_pieces)
    item_shard = lax.ppermute(item_shard, "rot", [(i, (i + 1) % n_rot) for i in range(n_rot)])
    tag_shard = stepped(shard_of(w, "rot"), tag_pieces)
    rotated_items = gathered(item_shard, "tag")
    new_tags = gathered(tag_shard, "rot")
    return (new_users, rotated_items, new_tags)


def solution(mesh):
    placed = (
        P(("rot", "tag"), None),
        P("rot", None),
        P("tag", None),
        P(("rot", "tag"), None),
        P(("rot", "tag")),
        P(("rot", "tag"), None, None),
        P(("rot", "tag"), None),
        P(("rot", "tag"), None, None),
    )
    return jax.shard_map(
        on_device,
        mesh=mesh,
        in_specs=placed,
        out_specs=(P(("rot", "tag"), None), P("rot", None), P("tag", None)),
        check_vma=False,
    )
```

```python
import jax
import jax.numpy as jnp
from jax import lax
from jax.experimental import pallas as pl
from jax.experimental.pallas import tpu as pltpu
from jax.sharding import PartitionSpec as P

TILE = 128
F32 = jnp.float32
BF16 = jnp.bfloat16


def tile(index):
    return pl.ds(pl.multiple_of(index * TILE, TILE), TILE)


def dot_rows(left, right):
    return lax.dot_general(left, right, (((1,), (1,)), ((), ())), preferred_element_type=F32)


def grads_kernel(
    rt_ref, rc_ref, xt_ref, core_ref, u_hbm, v_hbm, w_hbm, r_hbm, x_hbm,
    item_ref, send_ref, own_ref, err_ref,
    u_ref, v_ref, w_ref, r_ref, x_ref, err_t, tag_err, tag_err_t, sems,
):
    copies = [
        pltpu.make_async_copy(src, dst, sems.at[i])
        for i, (src, dst) in enumerate(
            [(v_hbm, v_ref), (w_hbm, w_ref), (x_hbm, x_ref), (u_hbm, u_ref), (r_hbm, r_ref)]
        )
    ]
    for copy in copies:
        copy.start()
    err_ref[...] = jnp.zeros_like(err_ref)
    err_t[...] = jnp.zeros_like(err_t)
    tag_err[...] = jnp.zeros_like(tag_err)
    tag_err_t[...] = jnp.zeros_like(tag_err_t)
    for copy in copies[:3]:
        copy.wait()
    for s in range(x_ref.shape[0]):
        a, c = tile(xt_ref[0, s]), tile(xt_ref[1, s])
        e = dot_rows(v_ref[a, :], w_ref[c, :]) - x_ref[s].astype(F32)
        tag_err[a, c] = e.astype(BF16)
        tag_err_t[c, a] = e.T.astype(BF16)
    for copy in copies[3:]:
        copy.wait()
    count = rc_ref[0]
    for s in range(r_ref.shape[0]):
        a, c = tile(rt_ref[0, s]), tile(rt_ref[1, s])
        e = dot_rows(u_ref[a, :], v_ref[c, :]) - r_ref[s].astype(F32)
        e = jnp.where(s < count, e, 0.0)
        err_ref[a, c] = e.astype(BF16)
        err_t[c, a] = e.T.astype(BF16)
    step = 256
    for i in range(0, item_ref.shape[0], step):
        rows = pl.ds(i, step)
        part = jnp.dot(err_t[rows, :], u_ref[...], preferred_element_type=F32)
        part += jnp.dot(tag_err[rows, :], w_ref[...], preferred_element_type=F32)
        item_ref[rows, :] = part.astype(BF16)
    half = own_ref.shape[0]
    core = core_ref[0]
    mine, other = (pl.ds(pl.multiple_of(h * half, half), half) for h in (core, 1 - core))
    own_ref[...] = jnp.dot(tag_err_t[mine, :], v_ref[...], preferred_element_type=F32)
    part = jnp.dot(tag_err_t[other, :], v_ref[...], preferred_element_type=F32)
    send_ref[...] = part.astype(BF16)


def users_kernel(err_ref, u_ref, v_ref, out_ref):
    step = 256
    for i in range(0, out_ref.shape[0], step):
        rows = pl.ds(i, step)
        grad = jnp.dot(err_ref[rows, :], v_ref[...], preferred_element_type=F32)
        old = u_ref[rows, :].astype(F32)
        out_ref[rows, :] = (old - 0.04 * (grad + 0.05 * old)).astype(BF16)


def whole():
    return pl.BlockSpec(memory_space=pltpu.VMEM)


def scalars():
    return pl.BlockSpec(memory_space=pltpu.SMEM)


def in_hbm():
    return pl.BlockSpec(memory_space=pltpu.HBM)


def partials(rt, rc, xt, core, u, v, w, r, x):
    users, rank = u.shape
    items, tags = v.shape[0], w.shape[0]
    return pl.pallas_call(
        grads_kernel,
        out_shape=(
            jax.ShapeDtypeStruct((items, rank), BF16),
            jax.ShapeDtypeStruct((tags // 2, rank), BF16),
            jax.ShapeDtypeStruct((tags // 2, rank), F32),
            jax.ShapeDtypeStruct((users, items), BF16),
        ),
        in_specs=[scalars()] * 4 + [in_hbm()] * 5,
        out_specs=(whole(),) * 4,
        scratch_shapes=[pltpu.VMEM(a.shape, BF16) for a in (u, v, w, r, x)]
        + [
            pltpu.VMEM((items, users), BF16),
            pltpu.VMEM((items, tags), BF16),
            pltpu.VMEM((tags, items), BF16),
            pltpu.SemaphoreType.DMA((5,)),
        ],
        compiler_params=pltpu.CompilerParams(vmem_limit_bytes=24 << 20),
        cost_estimate=pl.CostEstimate(flops=3 << 30, bytes_accessed=6 << 20, transcendentals=0),
    )(rt, rc, xt, core, *(pltpu.with_memory_space_constraint(a, pltpu.HBM) for a in (u, v, w, r, x)))


def updated_users(err, u, v):
    return pl.pallas_call(
        users_kernel,
        out_shape=jax.ShapeDtypeStruct(u.shape, BF16),
        in_specs=[whole()] * 3,
        out_specs=whole(),
        compiler_params=pltpu.CompilerParams(vmem_limit_bytes=16 << 20),
        cost_estimate=pl.CostEstimate(flops=1 << 30, bytes_accessed=4 << 20, transcendentals=0),
    )(err, u, v)


def exchanged(pieces, axis):
    return lax.all_to_all(pieces, axis, 0, 0)


def updated(old, total):
    old = old.astype(F32)
    return (old - 0.04 * (total + 0.05 * old)).astype(BF16)


def part_of(block, index, size):
    return lax.dynamic_slice_in_dim(block, index * size, size, 0)


def swapped(block, mask):
    n = lax.axis_size("rot")
    return lax.ppermute(block, "rot", [(i, i ^ mask) for i in range(n)])


def joined(mine, other, bit):
    return jnp.where(
        bit == 0, jnp.concatenate([mine, other], 0), jnp.concatenate([other, mine], 0)
    )


def added(own, mask):
    own = lax.reduce_precision(own, 8, 7)
    return own + swapped(own.astype(BF16), mask).astype(F32)


def tag_sum_in_plane(send, own, x_hi):
    own = own + swapped(send, 1).astype(F32)
    size = own.shape[0] // 2
    send = part_of(own, 1 - x_hi, size).astype(BF16)
    own = part_of(own, x_hi, size) + swapped(send, 2).astype(F32)
    return added(own, 4)


def new_tag_rows(total, w, core, x_hi):
    shard = updated(part_of(w, core * 2 + x_hi, total.shape[0]), total)
    half = joined(shard, swapped(shard, 2), x_hi)
    return joined(half, swapped(half, 1), core)


def on_device(u, v, w, rating_tiles, rating_counts, ratings, tag_tiles, tag_values):
    rank = u.shape[1]
    n_rot, n_tag = lax.axis_size("rot"), lax.axis_size("tag")
    rot = lax.axis_index("rot")
    core, x_hi = rot & 1, (rot >> 1) & 1
    item_part, tag_send, tag_own, err = partials(
        rating_tiles.T, rating_counts, tag_tiles.T, core[None], u, v, w, ratings, tag_values
    )
    item_pieces = exchanged(item_part.reshape(n_tag, -1, rank), "tag")
    new_users = updated_users(err, u, v)
    tag_total = tag_sum_in_plane(tag_send, tag_own, x_hi)
    item_pieces, tag_total, new_users = lax.optimization_barrier(
        (item_pieces, tag_total, new_users)
    )
    shard = part_of(v, lax.axis_index("tag"), v.shape[0] // n_tag)
    shard = updated(shard, jnp.sum(item_pieces.astype(F32), axis=0))
    shard = lax.ppermute(shard, "rot", [(i, (i + 1) % n_rot) for i in range(n_rot)])
    tag_total = added(tag_total, 8)
    shard, tag_total = lax.optimization_barrier((shard, tag_total))
    copies = jnp.broadcast_to(shard, (n_tag,) + shard.shape)
    rotated_items = exchanged(copies, "tag").reshape(v.shape)
    new_tags = new_tag_rows(added(tag_total, 16), w, core, x_hi)
    return (new_users, rotated_items, new_tags)


def solution(mesh):
    placed = (
        P(("rot", "tag"), None),
        P("rot", None),
        P("tag", None),
        P(("rot", "tag"), None),
        P(("rot", "tag")),
        P(("rot", "tag"), None, None),
        P(("rot", "tag"), None),
        P(("rot", "tag"), None, None),
    )
    return jax.shard_map(
        on_device,
        mesh=mesh,
        in_specs=placed,
        out_specs=(P(("rot", "tag"), None), P("rot", None), P("tag", None)),
        check_vma=False,
    )
```

```python
import jax
import jax.numpy as jnp
from jax import lax
from jax.experimental import pallas as pl
from jax.experimental.pallas import tpu as pltpu
from jax.sharding import PartitionSpec as P

TILE = 128
F32 = jnp.float32
BF16 = jnp.bfloat16


def tile(index):
    return pl.ds(pl.multiple_of(index * TILE, TILE), TILE)


def dot_rows(left, right):
    return lax.dot_general(left, right, (((1,), (1,)), ((), ())), preferred_element_type=F32)


def errors_kernel(
    rt_ref, rc_ref, xt_ref, u_hbm, v_hbm, w_hbm, r_hbm, x_hbm,
    item_a_ref, err_ref, err_t_b, tag_err_b, tag_err_t,
    u_ref, v_ref, w_ref, r_ref, x_ref, err_t, tag_err, sems,
):
    copies = [
        pltpu.make_async_copy(src, dst, sems.at[i])
        for i, (src, dst) in enumerate(
            [(v_hbm, v_ref), (w_hbm, w_ref), (x_hbm, x_ref), (u_hbm, u_ref), (r_hbm, r_ref)]
        )
    ]
    for copy in copies:
        copy.start()
    for ref in (err_ref, err_t, tag_err, tag_err_t):
        ref[...] = jnp.zeros_like(ref)
    for copy in copies[:3]:
        copy.wait()
    for s in range(x_ref.shape[0]):
        a, c = tile(xt_ref[0, s]), tile(xt_ref[1, s])
        e = dot_rows(v_ref[a, :], w_ref[c, :]) - x_ref[s].astype(F32)
        tag_err[a, c] = e.astype(BF16)
        tag_err_t[c, a] = e.T.astype(BF16)
    for copy in copies[3:]:
        copy.wait()
    count = rc_ref[0]
    for s in range(r_ref.shape[0]):
        a, c = tile(rt_ref[0, s]), tile(rt_ref[1, s])
        e = dot_rows(u_ref[a, :], v_ref[c, :]) - r_ref[s].astype(F32)
        e = jnp.where(s < count, e, 0.0)
        err_ref[a, c] = e.astype(BF16)
        err_t[c, a] = e.T.astype(BF16)
    half = item_a_ref.shape[0]
    step = 256
    for i in range(0, half, step):
        rows = pl.ds(i, step)
        part = jnp.dot(err_t[rows, :], u_ref[...], preferred_element_type=F32)
        part += jnp.dot(tag_err[rows, :], w_ref[...], preferred_element_type=F32)
        item_a_ref[rows, :] = part.astype(BF16)
    err_t_b[...] = err_t[half:, :]
    tag_err_b[...] = tag_err[half:, :]


def second_kernel(
    core_ref, x_lo_ref, err_t, tag_err, tag_err_t, u_ref, v_ref, w_ref,
    item_own, item_send, tag_own, tag_send,
):
    def halves(index, size):
        return (pl.ds(pl.multiple_of(h * size, size), size) for h in (index, 1 - index))

    mine, other = halves(core_ref[0], tag_own.shape[0])
    tag_own[...] = jnp.dot(tag_err_t[mine, :], v_ref[...], preferred_element_type=F32)
    part = jnp.dot(tag_err_t[other, :], v_ref[...], preferred_element_type=F32)
    tag_send[...] = part.astype(BF16)
    mine, other = halves(x_lo_ref[0], item_own.shape[0])
    part = jnp.dot(err_t[other, :], u_ref[...], preferred_element_type=F32)
    part += jnp.dot(tag_err[other, :], w_ref[...], preferred_element_type=F32)
    item_send[...] = part.astype(BF16)
    part = jnp.dot(err_t[mine, :], u_ref[...], preferred_element_type=F32)
    part += jnp.dot(tag_err[mine, :], w_ref[...], preferred_element_type=F32)
    item_own[...] = part


def users_kernel(err_ref, u_ref, v_ref, out_ref):
    step = 256
    for i in range(0, out_ref.shape[0], step):
        rows = pl.ds(i, step)
        grad = jnp.dot(err_ref[rows, :], v_ref[...], preferred_element_type=F32)
        old = u_ref[rows, :].astype(F32)
        out_ref[rows, :] = (old - 0.04 * (grad + 0.05 * old)).astype(BF16)


def whole():
    return pl.BlockSpec(memory_space=pltpu.VMEM)


def scalars():
    return pl.BlockSpec(memory_space=pltpu.SMEM)


def in_hbm():
    return pl.BlockSpec(memory_space=pltpu.HBM)


def like(*dims, dtype=BF16):
    return jax.ShapeDtypeStruct(dims, dtype)


def limits(mib):
    return pltpu.CompilerParams(vmem_limit_bytes=mib << 20)


def cost(flops, moved):
    return pl.CostEstimate(flops=flops, bytes_accessed=moved, transcendentals=0)


def errors(rt, rc, xt, u, v, w, r, x):
    users, rank = u.shape
    items, tags = v.shape[0], w.shape[0]
    half = items // 2
    return pl.pallas_call(
        errors_kernel,
        out_shape=(
            like(half, rank),
            like(users, items),
            like(half, users),
            like(half, tags),
            like(tags, items),
        ),
        in_specs=[scalars()] * 3 + [in_hbm()] * 5,
        out_specs=(whole(),) * 5,
        scratch_shapes=[pltpu.VMEM(a.shape, BF16) for a in (u, v, w, r, x)]
        + [
            pltpu.VMEM((items, users), BF16),
            pltpu.VMEM((items, tags), BF16),
            pltpu.SemaphoreType.DMA((5,)),
        ],
        compiler_params=limits(24),
        cost_estimate=cost(2 << 30, 6 << 20),
    )(rt, rc, xt, *(pltpu.with_memory_space_constraint(a, pltpu.HBM) for a in (u, v, w, r, x)))


def second_parts(core, x_lo, err_t, tag_err, tag_err_t, u, v, w):
    rank = u.shape[1]
    items, tags = err_t.shape[0] // 2, w.shape[0] // 2
    return pl.pallas_call(
        second_kernel,
        out_shape=(
            like(items, rank, dtype=F32),
            like(items, rank),
            like(tags, rank, dtype=F32),
            like(tags, rank),
        ),
        in_specs=[scalars()] * 2 + [whole()] * 6,
        out_specs=(whole(),) * 4,
        compiler_params=limits(16),
        cost_estimate=cost(1 << 30, 6 << 20),
    )(core, x_lo, err_t, tag_err, tag_err_t, u, v, w)


def updated_users(err, u, v):
    return pl.pallas_call(
        users_kernel,
        out_shape=like(*u.shape),
        in_specs=[whole()] * 3,
        out_specs=whole(),
        compiler_params=limits(16),
        cost_estimate=cost(1 << 30, 4 << 20),
    )(err, u, v)


def updated(old, total):
    old = old.astype(F32)
    return (old - 0.04 * (total + 0.05 * old)).astype(BF16)


def rows_from(block, start, size):
    return lax.dynamic_slice_in_dim(block, start, size, 0)


def swapped(block, mask, axis="rot"):
    n = lax.axis_size(axis)
    return lax.ppermute(block, axis, [(i, i ^ mask) for i in range(n)])


def rotated(block):
    n = lax.axis_size("rot")
    return lax.ppermute(block, "rot", [(i, (i + 1) % n) for i in range(n)])


def joined(mine, other, bit):
    return jnp.where(
        bit == 0, jnp.concatenate([mine, other], 0), jnp.concatenate([other, mine], 0)
    )


def added(own, mask):
    own = lax.reduce_precision(own, 8, 7)
    return own + swapped(own.astype(BF16), mask).astype(F32)


def tag_sum_in_plane(send, own, x_hi):
    own = own + swapped(send, 1).astype(F32)
    size = own.shape[0] // 2
    send = rows_from(own, (1 - x_hi) * size, size).astype(BF16)
    return rows_from(own, x_hi * size, size) + swapped(send, 2).astype(F32)


def new_tag_rows(total, w, core, x_hi):
    size = total.shape[0]
    shard = updated(rows_from(w, (core * 2 + x_hi) * size, size), total)
    half = joined(shard, swapped(shard, 2), x_hi)
    return joined(half, swapped(half, 1), core)


def total_of(pieces):
    return jnp.sum(pieces.astype(F32), axis=0)


def gathered(shard):
    copies = jnp.broadcast_to(shard, (lax.axis_size("tag"),) + shard.shape)
    return lax.all_to_all(copies, "tag", 0, 0)


def on_device(u, v, w, rating_tiles, rating_counts, ratings, tag_tiles, tag_values):
    items, rank = v.shape
    n_tag = lax.axis_size("tag")
    rot, tag = lax.axis_index("rot"), lax.axis_index("tag")
    core, x_hi = rot & 1, (rot >> 1) & 1
    x_lo, z = tag & 1, tag >> 1
    half, size = items // 2, items // 2 // n_tag
    columns = [[x + 2 * k for k in range(n_tag // 2)] for x in range(2)]

    item_a, err, err_t_b, tag_err_b, tag_err_t = errors(
        rating_tiles.T, rating_counts, tag_tiles.T, u, v, w, ratings, tag_values
    )
    pieces_a = lax.all_to_all(item_a.reshape(n_tag, size, rank), "tag", 0, 0)
    own_b, send_b, tag_own, tag_send = second_parts(
        core[None], x_lo[None], err_t_b, tag_err_b, tag_err_t, u, v, w
    )
    new_users = updated_users(err, u, v)
    tag_total = tag_sum_in_plane(tag_send, tag_own, x_hi)
    pair_b = (own_b + swapped(send_b, 1, "tag").astype(F32)).astype(BF16)
    pieces_a, pair_b, tag_total, new_users = lax.optimization_barrier(
        (pieces_a, pair_b, tag_total, new_users)
    )
    pieces_b = lax.all_to_all(
        pair_b.reshape(n_tag // 2, size, rank), "tag", 0, 0, axis_index_groups=columns
    )
    shard_a = rotated(updated(rows_from(v, tag * size, size), total_of(pieces_a)))
    tag_total = added(tag_total, 4)
    pieces_b, shard_a, tag_total = lax.optimization_barrier((pieces_b, shard_a, tag_total))
    new_a = gathered(shard_a)
    place = half + x_lo * (half // 2) + z * size
    shard_b = rotated(updated(rows_from(v, place, size), total_of(pieces_b)))
    tag_total = added(tag_total, 8)
    new_a, shard_b, tag_total = lax.optimization_barrier((new_a, shard_b, tag_total))
    new_b = gathered(shard_b)
    new_tags = new_tag_rows(added(tag_total, 16), w, core, x_hi)
    new_b = jnp.swapaxes(new_b.reshape(n_tag // 2, 2, size, rank), 0, 1)
    rotated_items = jnp.concatenate([new_a.reshape(half, rank), new_b.reshape(half, rank)], 0)
    return (new_users, rotated_items, new_tags)


def solution(mesh):
    placed = (
        P(("rot", "tag"), None),
        P("rot", None),
        P("tag", None),
        P(("rot", "tag"), None),
        P(("rot", "tag")),
        P(("rot", "tag"), None, None),
        P(("rot", "tag"), None),
        P(("rot", "tag"), None, None),
    )
    return jax.shard_map(
        on_device,
        mesh=mesh,
        in_specs=placed,
        out_specs=(P(("rot", "tag"), None), P("rot", None), P("tag", None)),
        check_vma=False,
    )
```

```python
import jax
import jax.numpy as jnp
from jax import lax
from jax.experimental import pallas as pl
from jax.experimental.pallas import tpu as pltpu
from jax.sharding import PartitionSpec as P

TILE = 128
F32 = jnp.float32
BF16 = jnp.bfloat16


def tile(index):
    return pl.ds(pl.multiple_of(index * TILE, TILE), TILE)


def dot_rows(left, right):
    return lax.dot_general(left, right, (((1,), (1,)), ((), ())), preferred_element_type=F32)


def grads_kernel(
    rc_ref, core_ref, xt_hbm, rt_hbm, u_hbm, v_hbm, w_hbm, r_hbm, x_hbm,
    item_ref, send_ref, own_ref, err_ref,
    xt_ref, rt_ref, u_ref, v_ref, w_ref, r_ref, x_ref, err_t, tag_err, tag_err_t, sems,
):
    copies = [
        pltpu.make_async_copy(src, dst, sems.at[i])
        for i, (src, dst) in enumerate(
            [
                (xt_hbm, xt_ref), (v_hbm, v_ref), (w_hbm, w_ref), (x_hbm, x_ref),
                (rt_hbm, rt_ref), (u_hbm, u_ref), (r_hbm, r_ref),
            ]
        )
    ]
    for copy in copies:
        copy.start()
    err_ref[...] = jnp.zeros_like(err_ref)
    err_t[...] = jnp.zeros_like(err_t)
    tag_err[...] = jnp.zeros_like(tag_err)
    tag_err_t[...] = jnp.zeros_like(tag_err_t)
    for copy in copies[:4]:
        copy.wait()
    for s in range(x_ref.shape[0]):
        a, c = tile(xt_ref[0, s]), tile(xt_ref[1, s])
        e = dot_rows(v_ref[a, :], w_ref[c, :]) - x_ref[s].astype(F32)
        tag_err[a, c] = e.astype(BF16)
        tag_err_t[c, a] = e.T.astype(BF16)
    for copy in copies[4:]:
        copy.wait()
    count = rc_ref[0]
    for s in range(r_ref.shape[0]):
        a, c = tile(rt_ref[0, s]), tile(rt_ref[1, s])
        e = dot_rows(u_ref[a, :], v_ref[c, :]) - r_ref[s].astype(F32)
        e = jnp.where(s < count, e, 0.0)
        err_ref[a, c] = e.astype(BF16)
        err_t[c, a] = e.T.astype(BF16)
    step = 256
    for i in range(0, item_ref.shape[0], step):
        rows = pl.ds(i, step)
        part = jnp.dot(err_t[rows, :], u_ref[...], preferred_element_type=F32)
        part += jnp.dot(tag_err[rows, :], w_ref[...], preferred_element_type=F32)
        item_ref[rows, :] = part.astype(BF16)
    half = own_ref.shape[0]
    core = core_ref[0]
    mine, other = (pl.ds(pl.multiple_of(h * half, half), half) for h in (core, 1 - core))
    own_ref[...] = jnp.dot(tag_err_t[mine, :], v_ref[...], preferred_element_type=F32)
    part = jnp.dot(tag_err_t[other, :], v_ref[...], preferred_element_type=F32)
    send_ref[...] = part.astype(BF16)


def users_kernel(err_ref, u_ref, v_ref, out_ref):
    step = 256
    for i in range(0, out_ref.shape[0], step):
        rows = pl.ds(i, step)
        grad = jnp.dot(err_ref[rows, :], v_ref[...], preferred_element_type=F32)
        old = u_ref[rows, :].astype(F32)
        out_ref[rows, :] = (old - 0.04 * (grad + 0.05 * old)).astype(BF16)


def split_kernel(bit_ref, own_ref, arrived_ref, keep_ref, send_ref):
    size = keep_ref.shape[0]
    mine, other = (
        pl.ds(pl.multiple_of(h * size, size), size) for h in (bit_ref[0], 1 - bit_ref[0])
    )
    keep_ref[...] = own_ref[mine, :] + arrived_ref[mine, :].astype(F32)
    send_ref[...] = (own_ref[other, :] + arrived_ref[other, :].astype(F32)).astype(BF16)


def whole():
    return pl.BlockSpec(memory_space=pltpu.VMEM)


def scalars():
    return pl.BlockSpec(memory_space=pltpu.SMEM)


def in_hbm():
    return pl.BlockSpec(memory_space=pltpu.HBM)


def partials(rt, rc, xt, core, u, v, w, r, x):
    users, rank = u.shape
    items, tags = v.shape[0], w.shape[0]
    return pl.pallas_call(
        grads_kernel,
        out_shape=(
            jax.ShapeDtypeStruct((items, rank), BF16),
            jax.ShapeDtypeStruct((tags // 2, rank), BF16),
            jax.ShapeDtypeStruct((tags // 2, rank), F32),
            jax.ShapeDtypeStruct((users, items), BF16),
        ),
        in_specs=[scalars()] * 2 + [in_hbm()] * 7,
        out_specs=(whole(),) * 4,
        scratch_shapes=[pltpu.SMEM(a.shape, a.dtype) for a in (xt, rt)]
        + [pltpu.VMEM(a.shape, BF16) for a in (u, v, w, r, x)]
        + [
            pltpu.VMEM((items, users), BF16),
            pltpu.VMEM((items, tags), BF16),
            pltpu.VMEM((tags, items), BF16),
            pltpu.SemaphoreType.DMA((7,)),
        ],
        compiler_params=pltpu.CompilerParams(vmem_limit_bytes=24 << 20),
        cost_estimate=pl.CostEstimate(flops=3 << 30, bytes_accessed=6 << 20, transcendentals=0),
    )(rc, core, *(pltpu.with_memory_space_constraint(a, pltpu.HBM) for a in (xt, rt, u, v, w, r, x)))


def updated_users(err, u, v):
    return pl.pallas_call(
        users_kernel,
        out_shape=jax.ShapeDtypeStruct(u.shape, BF16),
        in_specs=[whole()] * 3,
        out_specs=whole(),
        compiler_params=pltpu.CompilerParams(vmem_limit_bytes=16 << 20),
        cost_estimate=pl.CostEstimate(flops=1 << 30, bytes_accessed=4 << 20, transcendentals=0),
    )(err, u, v)


def split_sum(bit, own, arrived):
    size, rank = own.shape[0] // 2, own.shape[1]
    return pl.pallas_call(
        split_kernel,
        out_shape=(
            jax.ShapeDtypeStruct((size, rank), F32),
            jax.ShapeDtypeStruct((size, rank), BF16),
        ),
        in_specs=[scalars(), whole(), whole()],
        out_specs=(whole(),) * 2,
        compiler_params=pltpu.CompilerParams(vmem_limit_bytes=4 << 20),
        cost_estimate=pl.CostEstimate(flops=1 << 18, bytes_accessed=1 << 20, transcendentals=0),
    )(bit, own, arrived)


def exchanged(pieces, axis):
    return lax.all_to_all(pieces, axis, 0, 0)


def updated(old, total):
    old = old.astype(F32)
    return (old - 0.04 * (total + 0.05 * old)).astype(BF16)


def part_of(block, index, size):
    return lax.dynamic_slice_in_dim(block, index * size, size, 0)


def swapped(block, mask):
    n = lax.axis_size("rot")
    return lax.ppermute(block, "rot", [(i, i ^ mask) for i in range(n)])


def joined(mine, other, bit):
    return jnp.where(
        bit == 0, jnp.concatenate([mine, other], 0), jnp.concatenate([other, mine], 0)
    )


def added(own, mask):
    own = lax.reduce_precision(own, 8, 7)
    return own + swapped(own.astype(BF16), mask).astype(F32)


def tag_sum_in_plane(send, own, x_hi):
    own, send = split_sum(x_hi[None], own, swapped(send, 1))
    return added(own + swapped(send, 2).astype(F32), 4)


def new_tag_rows(total, w, core, x_hi):
    shard = updated(part_of(w, core * 2 + x_hi, total.shape[0]), total)
    half = joined(shard, swapped(shard, 2), x_hi)
    return joined(half, swapped(half, 1), core)


def on_device(u, v, w, rating_tiles, rating_counts, ratings, tag_tiles, tag_values):
    rank = u.shape[1]
    n_rot, n_tag = lax.axis_size("rot"), lax.axis_size("tag")
    rot = lax.axis_index("rot")
    core, x_hi = rot & 1, (rot >> 1) & 1
    item_part, tag_send, tag_own, err = partials(
        rating_tiles.T, rating_counts, tag_tiles.T, core[None], u, v, w, ratings, tag_values
    )
    item_pieces = exchanged(item_part.reshape(n_tag, -1, rank), "tag")
    tag_total = tag_sum_in_plane(tag_send, tag_own, x_hi)
    item_pieces, _ = lax.optimization_barrier((item_pieces, tag_total))
    shard = part_of(v, lax.axis_index("tag"), v.shape[0] // n_tag)
    shard = updated(shard, jnp.sum(item_pieces.astype(F32), axis=0))
    shard = lax.ppermute(shard, "rot", [(i, (i + 1) % n_rot) for i in range(n_rot)])
    tag_total = added(tag_total, 8)
    shard, err, _ = lax.optimization_barrier((shard, err, tag_total))
    new_users = updated_users(err, u, v)
    copies = jnp.broadcast_to(shard, (n_tag,) + shard.shape)
    rotated_items = exchanged(copies, "tag").reshape(v.shape)
    new_tags = new_tag_rows(added(tag_total, 16), w, core, x_hi)
    return (new_users, rotated_items, new_tags)


def solution(mesh):
    placed = (
        P(("rot", "tag"), None),
        P("rot", None),
        P("tag", None),
        P(("rot", "tag"), None),
        P(("rot", "tag")),
        P(("rot", "tag"), None, None),
        P(("rot", "tag"), None),
        P(("rot", "tag"), None, None),
    )
    return jax.shard_map(
        on_device,
        mesh=mesh,
        in_specs=placed,
        out_specs=(P(("rot", "tag"), None), P("rot", None), P("tag", None)),
        check_vma=False,
    )
```

```python
import jax
import jax.numpy as jnp
from jax import lax
from jax.experimental import pallas as pl
from jax.experimental.pallas import tpu as pltpu
from jax.sharding import PartitionSpec as P

TILE = 128
F32 = jnp.float32
BF16 = jnp.bfloat16


def tile(index):
    return pl.ds(pl.multiple_of(index * TILE, TILE), TILE)


def dot_rows(left, right):
    return lax.dot_general(left, right, (((1,), (1,)), ((), ())), preferred_element_type=F32)


def grads_kernel(
    rc_ref, core_ref, xt_hbm, rt_hbm, u_hbm, v_hbm, w_hbm, r_hbm, x_hbm,
    item_ref, send_ref, own_ref, err_ref,
    xt_ref, rt_ref, u_ref, v_ref, w_ref, r_ref, x_ref, err_t, tag_err, tag_err_t, sems,
):
    copies = [
        pltpu.make_async_copy(src, dst, sems.at[i])
        for i, (src, dst) in enumerate(
            [
                (xt_hbm, xt_ref), (v_hbm, v_ref), (w_hbm, w_ref), (x_hbm, x_ref),
                (rt_hbm, rt_ref), (u_hbm, u_ref), (r_hbm, r_ref),
            ]
        )
    ]
    for copy in copies:
        copy.start()
    err_ref[...] = jnp.zeros_like(err_ref)
    err_t[...] = jnp.zeros_like(err_t)
    tag_err[...] = jnp.zeros_like(tag_err)
    tag_err_t[...] = jnp.zeros_like(tag_err_t)
    for copy in copies[:4]:
        copy.wait()
    for s in range(x_ref.shape[0]):
        a, c = tile(xt_ref[0, s]), tile(xt_ref[1, s])
        e = dot_rows(v_ref[a, :], w_ref[c, :]) - x_ref[s].astype(F32)
        tag_err[a, c] = e.astype(BF16)
        tag_err_t[c, a] = e.T.astype(BF16)
    for copy in copies[4:]:
        copy.wait()
    count = rc_ref[0]
    for s in range(r_ref.shape[0]):
        a, c = tile(rt_ref[0, s]), tile(rt_ref[1, s])
        e = dot_rows(u_ref[a, :], v_ref[c, :]) - r_ref[s].astype(F32)
        e = jnp.where(s < count, e, 0.0)
        err_ref[a, c] = e.astype(BF16)
        err_t[c, a] = e.T.astype(BF16)
    step = 256
    for i in range(0, item_ref.shape[0], step):
        rows = pl.ds(i, step)
        part = jnp.dot(err_t[rows, :], u_ref[...], preferred_element_type=F32)
        part += jnp.dot(tag_err[rows, :], w_ref[...], preferred_element_type=F32)
        item_ref[rows, :] = part.astype(BF16)
    half = own_ref.shape[0]
    core = core_ref[0]
    mine, other = (pl.ds(pl.multiple_of(h * half, half), half) for h in (core, 1 - core))
    own_ref[...] = jnp.dot(tag_err_t[mine, :], v_ref[...], preferred_element_type=F32)
    part = jnp.dot(tag_err_t[other, :], v_ref[...], preferred_element_type=F32)
    send_ref[...] = part.astype(BF16)


def users_kernel(err_ref, u_ref, v_ref, out_ref):
    step = 256
    for i in range(0, out_ref.shape[0], step):
        rows = pl.ds(i, step)
        grad = jnp.dot(err_ref[rows, :], v_ref[...], preferred_element_type=F32)
        old = u_ref[rows, :].astype(F32)
        out_ref[rows, :] = (old - 0.04 * (grad + 0.05 * old)).astype(BF16)


def split_kernel(bit_ref, own_ref, arrived_ref, keep_ref, send_ref):
    size = keep_ref.shape[0]
    mine, other = (
        pl.ds(pl.multiple_of(h * size, size), size) for h in (bit_ref[0], 1 - bit_ref[0])
    )
    keep_ref[...] = own_ref[mine, :] + arrived_ref[mine, :].astype(F32)
    send_ref[...] = (own_ref[other, :] + arrived_ref[other, :].astype(F32)).astype(BF16)


def whole():
    return pl.BlockSpec(memory_space=pltpu.VMEM)


def scalars():
    return pl.BlockSpec(memory_space=pltpu.SMEM)


def in_hbm():
    return pl.BlockSpec(memory_space=pltpu.HBM)


def partials(rt, rc, xt, core, u, v, w, r, x):
    users, rank = u.shape
    items, tags = v.shape[0], w.shape[0]
    return pl.pallas_call(
        grads_kernel,
        out_shape=(
            jax.ShapeDtypeStruct((items, rank), BF16),
            jax.ShapeDtypeStruct((tags // 2, rank), BF16),
            jax.ShapeDtypeStruct((tags // 2, rank), F32),
            jax.ShapeDtypeStruct((users, items), BF16),
        ),
        in_specs=[scalars()] * 2 + [in_hbm()] * 7,
        out_specs=(whole(),) * 4,
        scratch_shapes=[pltpu.SMEM(a.shape, a.dtype) for a in (xt, rt)]
        + [pltpu.VMEM(a.shape, BF16) for a in (u, v, w, r, x)]
        + [
            pltpu.VMEM((items, users), BF16),
            pltpu.VMEM((items, tags), BF16),
            pltpu.VMEM((tags, items), BF16),
            pltpu.SemaphoreType.DMA((7,)),
        ],
        compiler_params=pltpu.CompilerParams(vmem_limit_bytes=24 << 20),
        cost_estimate=pl.CostEstimate(flops=3 << 30, bytes_accessed=6 << 20, transcendentals=0),
    )(rc, core, *(pltpu.with_memory_space_constraint(a, pltpu.HBM) for a in (xt, rt, u, v, w, r, x)))


def updated_users(err, u, v):
    return pl.pallas_call(
        users_kernel,
        out_shape=jax.ShapeDtypeStruct(u.shape, BF16),
        in_specs=[whole()] * 3,
        out_specs=whole(),
        compiler_params=pltpu.CompilerParams(vmem_limit_bytes=8 << 20),
        cost_estimate=pl.CostEstimate(flops=1 << 30, bytes_accessed=4 << 20, transcendentals=0),
    )(err, u, v)


def split_sum(bit, own, arrived):
    size, rank = own.shape[0] // 2, own.shape[1]
    return pl.pallas_call(
        split_kernel,
        out_shape=(
            jax.ShapeDtypeStruct((size, rank), F32),
            jax.ShapeDtypeStruct((size, rank), BF16),
        ),
        in_specs=[scalars(), whole(), whole()],
        out_specs=(whole(),) * 2,
        compiler_params=pltpu.CompilerParams(vmem_limit_bytes=4 << 20),
        cost_estimate=pl.CostEstimate(flops=1 << 18, bytes_accessed=1 << 20, transcendentals=0),
    )(bit, own, arrived)


def exchanged(pieces, axis):
    return lax.all_to_all(pieces, axis, 0, 0)


def updated(old, total):
    old = old.astype(F32)
    return (old - 0.04 * (total + 0.05 * old)).astype(BF16)


def part_of(block, index, size):
    return lax.dynamic_slice_in_dim(block, index * size, size, 0)


def swapped(block, mask):
    n = lax.axis_size("rot")
    return lax.ppermute(block, "rot", [(i, i ^ mask) for i in range(n)])


def joined(mine, other, bit):
    return jnp.where(
        bit == 0, jnp.concatenate([mine, other], 0), jnp.concatenate([other, mine], 0)
    )


def added(own, mask):
    own = lax.reduce_precision(own, 8, 7)
    return own + swapped(own.astype(BF16), mask).astype(F32)


def tag_sum_in_plane(send, own, x_hi):
    own, send = split_sum(x_hi[None], own, swapped(send, 1))
    own = added(own + swapped(send, 2).astype(F32), 4)
    return added(own, 8)


def new_tag_rows(total, w, core, x_hi):
    shard = updated(part_of(w, core * 2 + x_hi, total.shape[0]), total)
    half = joined(shard, swapped(shard, 2), x_hi)
    return joined(half, swapped(half, 1), core)


def on_device(u, v, w, rating_tiles, rating_counts, ratings, tag_tiles, tag_values):
    rank = u.shape[1]
    n_rot, n_tag = lax.axis_size("rot"), lax.axis_size("tag")
    rot = lax.axis_index("rot")
    core, x_hi = rot & 1, (rot >> 1) & 1
    item_part, tag_send, tag_own, err = partials(
        rating_tiles.T, rating_counts, tag_tiles.T, core[None], u, v, w, ratings, tag_values
    )
    item_pieces = exchanged(item_part.reshape(n_tag, -1, rank), "tag")
    tag_total = tag_sum_in_plane(tag_send, tag_own, x_hi)
    item_pieces, tag_total = lax.optimization_barrier((item_pieces, tag_total))
    shard = part_of(v, lax.axis_index("tag"), v.shape[0] // n_tag)
    shard = updated(shard, jnp.sum(item_pieces.astype(F32), axis=0))
    shard = lax.ppermute(shard, "rot", [(i, (i + 1) % n_rot) for i in range(n_rot)])
    tag_total = added(tag_total, 16)
    shard, err, tag_total = lax.optimization_barrier((shard, err, tag_total))
    new_users = updated_users(err, u, v)
    copies = jnp.broadcast_to(shard, (n_tag,) + shard.shape)
    rotated_items = exchanged(copies, "tag").reshape(v.shape)
    new_tags = new_tag_rows(tag_total, w, core, x_hi)
    return (new_users, rotated_items, new_tags)


def solution(mesh):
    placed = (
        P(("rot", "tag"), None),
        P("rot", None),
        P("tag", None),
        P(("rot", "tag"), None),
        P(("rot", "tag")),
        P(("rot", "tag"), None, None),
        P(("rot", "tag"), None),
        P(("rot", "tag"), None, None),
    )
    return jax.shard_map(
        on_device,
        mesh=mesh,
        in_specs=placed,
        out_specs=(P(("rot", "tag"), None), P("rot", None), P("tag", None)),
        check_vma=False,
    )
```

```python
import jax
import jax.numpy as jnp
from jax import lax
from jax.experimental import pallas as pl
from jax.experimental.pallas import tpu as pltpu
from jax.sharding import PartitionSpec as P

TILE = 128
F32 = jnp.float32
BF16 = jnp.bfloat16


def tile(index):
    return pl.ds(pl.multiple_of(index * TILE, TILE), TILE)


def dot_rows(left, right):
    return lax.dot_general(left, right, (((1,), (1,)), ((), ())), preferred_element_type=F32)


def dot_cols(left, right):
    return lax.dot_general(left, right, (((0,), (0,)), ((), ())), preferred_element_type=F32)


def grads_kernel(
    rc_ref, core_ref, xt_hbm, rt_hbm, u_hbm, v_hbm, w_hbm, r_hbm, x_hbm,
    item_ref, send_ref, own_ref, err_ref,
    xt_ref, rt_ref, u_ref, v_ref, w_ref, r_ref, x_ref, tag_err, sems,
):
    copies = [
        pltpu.make_async_copy(src, dst, sems.at[i])
        for i, (src, dst) in enumerate(
            [
                (xt_hbm, xt_ref), (v_hbm, v_ref), (w_hbm, w_ref), (x_hbm, x_ref),
                (rt_hbm, rt_ref), (u_hbm, u_ref), (r_hbm, r_ref),
            ]
        )
    ]
    for copy in copies:
        copy.start()
    err_ref[...] = jnp.zeros_like(err_ref)
    tag_err[...] = jnp.zeros_like(tag_err)
    for copy in copies[:4]:
        copy.wait()
    for s in range(x_ref.shape[0]):
        a, c = tile(xt_ref[0, s]), tile(xt_ref[1, s])
        e = dot_rows(v_ref[a, :], w_ref[c, :]) - x_ref[s].astype(F32)
        tag_err[a, c] = e.astype(BF16)
    for copy in copies[4:]:
        copy.wait()
    count = rc_ref[0]
    for s in range(r_ref.shape[0]):
        a, c = tile(rt_ref[0, s]), tile(rt_ref[1, s])
        e = dot_rows(u_ref[a, :], v_ref[c, :]) - r_ref[s].astype(F32)
        e = jnp.where(s < count, e, 0.0)
        err_ref[a, c] = e.astype(BF16)
    step = 256
    for i in range(0, item_ref.shape[0], step):
        rows = pl.ds(i, step)
        part = dot_cols(err_ref[:, rows], u_ref[...])
        part += jnp.dot(tag_err[rows, :], w_ref[...], preferred_element_type=F32)
        item_ref[rows, :] = part.astype(BF16)
    half = own_ref.shape[0]
    core = core_ref[0]
    mine, other = (pl.ds(pl.multiple_of(h * half, half), half) for h in (core, 1 - core))
    own_ref[...] = dot_cols(tag_err[:, mine], v_ref[...])
    part = dot_cols(tag_err[:, other], v_ref[...])
    send_ref[...] = part.astype(BF16)


def users_kernel(err_ref, u_ref, v_ref, out_ref):
    step = 256
    for i in range(0, out_ref.shape[0], step):
        rows = pl.ds(i, step)
        grad = jnp.dot(err_ref[rows, :], v_ref[...], preferred_element_type=F32)
        old = u_ref[rows, :].astype(F32)
        out_ref[rows, :] = (old - 0.04 * (grad + 0.05 * old)).astype(BF16)


def split_kernel(bit_ref, own_ref, arrived_ref, keep_ref, send_ref):
    size = keep_ref.shape[0]
    mine, other = (
        pl.ds(pl.multiple_of(h * size, size), size) for h in (bit_ref[0], 1 - bit_ref[0])
    )
    keep_ref[...] = own_ref[mine, :] + arrived_ref[mine, :].astype(F32)
    send_ref[...] = (own_ref[other, :] + arrived_ref[other, :].astype(F32)).astype(BF16)


def item_kernel(tag_ref, v_hbm, pieces_hbm, out_ref, old_ref, pieces_ref, sems):
    count, size = pieces_ref.shape[:2]
    group = count // 4
    start = pl.multiple_of(tag_ref[0] * size, size)
    copies = [
        pltpu.make_async_copy(
            pieces_hbm.at[pl.ds(g * group, group)], pieces_ref.at[pl.ds(g * group, group)], sems.at[g]
        )
        for g in range(4)
    ]
    copies.append(pltpu.make_async_copy(v_hbm.at[pl.ds(start, size)], old_ref, sems.at[4]))
    for copy in copies:
        copy.start()
    total = jnp.zeros(out_ref.shape, F32)
    for g in range(4):
        copies[g].wait()
        for k in range(g * group, (g + 1) * group):
            total += pieces_ref[k].astype(F32)
    copies[4].wait()
    old = old_ref[...].astype(F32)
    out_ref[...] = (old - 0.04 * (total + 0.05 * old)).astype(BF16)


def spread_kernel(shard_ref, out_hbm, sems):
    copies = [
        pltpu.make_async_copy(shard_ref, out_hbm.at[k], sems.at[k])
        for k in range(out_hbm.shape[0])
    ]
    for copy in copies:
        copy.start()
    for copy in copies:
        copy.wait()


def place_kernel(in_ref, out_ref, sems):
    copies = [
        pltpu.make_async_copy(in_ref.at[k], out_ref.at[k], sems.at[k])
        for k in range(out_ref.shape[0])
    ]
    for copy in copies:
        copy.start()
    for copy in copies:
        copy.wait()


def whole():
    return pl.BlockSpec(memory_space=pltpu.VMEM)


def scalars():
    return pl.BlockSpec(memory_space=pltpu.SMEM)


def in_hbm():
    return pl.BlockSpec(memory_space=pltpu.HBM)


def partials(rt, rc, xt, core, u, v, w, r, x):
    users, rank = u.shape
    items, tags = v.shape[0], w.shape[0]
    return pl.pallas_call(
        grads_kernel,
        out_shape=(
            jax.ShapeDtypeStruct((items, rank), BF16),
            jax.ShapeDtypeStruct((tags // 2, rank), BF16),
            jax.ShapeDtypeStruct((tags // 2, rank), F32),
            jax.ShapeDtypeStruct((users, items), BF16),
        ),
        in_specs=[scalars()] * 2 + [in_hbm()] * 7,
        out_specs=(whole(),) * 4,
        scratch_shapes=[pltpu.SMEM(a.shape, a.dtype) for a in (xt, rt)]
        + [pltpu.VMEM(a.shape, BF16) for a in (u, v, w, r, x)]
        + [
            pltpu.VMEM((items, tags), BF16),
            pltpu.SemaphoreType.DMA((7,)),
        ],
        compiler_params=pltpu.CompilerParams(vmem_limit_bytes=14 << 20),
        cost_estimate=pl.CostEstimate(flops=3 << 30, bytes_accessed=6 << 20, transcendentals=0),
    )(rc, core, *(pltpu.with_memory_space_constraint(a, pltpu.HBM) for a in (xt, rt, u, v, w, r, x)))


def updated_users(err, u, v):
    return pl.pallas_call(
        users_kernel,
        out_shape=jax.ShapeDtypeStruct(u.shape, BF16),
        in_specs=[whole()] * 3,
        out_specs=whole(),
        compiler_params=pltpu.CompilerParams(vmem_limit_bytes=6 << 20),
        cost_estimate=pl.CostEstimate(flops=1 << 30, bytes_accessed=4 << 20, transcendentals=0),
    )(err, u, v)


def split_sum(bit, own, arrived):
    size, rank = own.shape[0] // 2, own.shape[1]
    return pl.pallas_call(
        split_kernel,
        out_shape=(
            jax.ShapeDtypeStruct((size, rank), F32),
            jax.ShapeDtypeStruct((size, rank), BF16),
        ),
        in_specs=[scalars(), whole(), whole()],
        out_specs=(whole(),) * 2,
        compiler_params=pltpu.CompilerParams(vmem_limit_bytes=4 << 20),
        cost_estimate=pl.CostEstimate(flops=1 << 18, bytes_accessed=1 << 20, transcendentals=0),
    )(bit, own, arrived)


def updated_items(tag, v, pieces):
    count, size, rank = pieces.shape
    return pl.pallas_call(
        item_kernel,
        out_shape=jax.ShapeDtypeStruct((size, rank), BF16),
        in_specs=[scalars(), in_hbm(), in_hbm()],
        out_specs=whole(),
        scratch_shapes=[
            pltpu.VMEM((size, rank), BF16),
            pltpu.VMEM(pieces.shape, BF16),
            pltpu.SemaphoreType.DMA((5,)),
        ],
        compiler_params=pltpu.CompilerParams(vmem_limit_bytes=4 << 20),
        cost_estimate=pl.CostEstimate(flops=1 << 19, bytes_accessed=1 << 20, transcendentals=0),
    )(tag, *(pltpu.with_memory_space_constraint(a, pltpu.HBM) for a in (v, pieces)))


def spread(shard, count):
    return pl.pallas_call(
        spread_kernel,
        out_shape=jax.ShapeDtypeStruct((count,) + shard.shape, BF16),
        in_specs=[whole()],
        out_specs=in_hbm(),
        scratch_shapes=[pltpu.SemaphoreType.DMA((count,))],
        compiler_params=pltpu.CompilerParams(vmem_limit_bytes=2 << 20),
        cost_estimate=pl.CostEstimate(flops=0, bytes_accessed=1 << 20, transcendentals=0),
    )(shard)


def placed_items(pieces):
    return pl.pallas_call(
        place_kernel,
        out_shape=jax.ShapeDtypeStruct(pieces.shape, BF16),
        in_specs=[pl.BlockSpec(memory_space=pl.ANY)],
        out_specs=in_hbm(),
        scratch_shapes=[pltpu.SemaphoreType.DMA((pieces.shape[0],))],
        compiler_params=pltpu.CompilerParams(vmem_limit_bytes=2 << 20),
        cost_estimate=pl.CostEstimate(flops=0, bytes_accessed=2 << 20, transcendentals=0),
    )(pieces)


def exchanged(pieces, axis):
    return lax.all_to_all(pieces, axis, 0, 0)


def updated(old, total):
    old = old.astype(F32)
    return (old - 0.04 * (total + 0.05 * old)).astype(BF16)


def part_of(block, index, size):
    return lax.dynamic_slice_in_dim(block, index * size, size, 0)


def swapped(block, mask):
    n = lax.axis_size("rot")
    return lax.ppermute(block, "rot", [(i, i ^ mask) for i in range(n)])


def joined(mine, other, bit):
    return jnp.where(
        bit == 0, jnp.concatenate([mine, other], 0), jnp.concatenate([other, mine], 0)
    )


def added(own, mask):
    own = lax.reduce_precision(own, 8, 7)
    return own + swapped(own.astype(BF16), mask).astype(F32)


def tag_sum_in_plane(send, own, x_hi):
    own, send = split_sum(x_hi[None], own, swapped(send, 1))
    return added(own + swapped(send, 2).astype(F32), 4)


def new_tag_rows(total, w, core, x_hi):
    shard = updated(part_of(w, core * 2 + x_hi, total.shape[0]), total)
    half = joined(shard, swapped(shard, 2), x_hi)
    return joined(half, swapped(half, 1), core)


def on_device(u, v, w, rating_tiles, rating_counts, ratings, tag_tiles, tag_values):
    rank = u.shape[1]
    n_rot, n_tag = lax.axis_size("rot"), lax.axis_size("tag")
    rot = lax.axis_index("rot")
    core, x_hi = rot & 1, (rot >> 1) & 1
    item_part, tag_send, tag_own, err = partials(
        rating_tiles.T, rating_counts, tag_tiles.T, core[None], u, v, w, ratings, tag_values
    )
    item_pieces = exchanged(item_part.reshape(n_tag, -1, rank), "tag")
    new_users = updated_users(err, u, v)
    tag_total = tag_sum_in_plane(tag_send, tag_own, x_hi)
    item_pieces, _, _ = lax.optimization_barrier((item_pieces, tag_total, new_users))
    shard = updated_items(lax.axis_index("tag")[None], v, item_pieces)
    shard = lax.ppermute(shard, "rot", [(i, (i + 1) % n_rot) for i in range(n_rot)])
    tag_total = added(tag_total, 8)
    shard, _ = lax.optimization_barrier((shard, tag_total))
    rotated_items = placed_items(exchanged(spread(shard, n_tag), "tag")).reshape(v.shape)
    new_tags = new_tag_rows(added(tag_total, 16), w, core, x_hi)
    return (new_users, rotated_items, new_tags)


def solution(mesh):
    placed = (
        P(("rot", "tag"), None),
        P("rot", None),
        P("tag", None),
        P(("rot", "tag"), None),
        P(("rot", "tag")),
        P(("rot", "tag"), None, None),
        P(("rot", "tag"), None),
        P(("rot", "tag"), None, None),
    )
    return jax.shard_map(
        on_device,
        mesh=mesh,
        in_specs=placed,
        out_specs=(P(("rot", "tag"), None), P("rot", None), P("tag", None)),
        check_vma=False,
    )
```

```python
import jax
import jax.numpy as jnp
from jax import lax
from jax.experimental import pallas as pl
from jax.experimental.pallas import tpu as pltpu
from jax.sharding import PartitionSpec as P

TILE = 128
F32 = jnp.float32
BF16 = jnp.bfloat16


def tile(index):
    return pl.ds(pl.multiple_of(index * TILE, TILE), TILE)


def dot_rows(left, right):
    return lax.dot_general(left, right, (((1,), (1,)), ((), ())), preferred_element_type=F32)


def dot_cols(left, right):
    return lax.dot_general(left, right, (((0,), (0,)), ((), ())), preferred_element_type=F32)


def grads_kernel(
    rc_ref, core_ref, xt_hbm, rt_hbm, u_hbm, v_hbm, w_hbm, r_hbm, x_hbm,
    item_ref, send_ref, own_ref, err_ref,
    xt_ref, rt_ref, u_ref, v_ref, w_ref, r_ref, x_ref, tag_err, sems,
):
    copies = [
        pltpu.make_async_copy(src, dst, sems.at[i])
        for i, (src, dst) in enumerate(
            [
                (xt_hbm, xt_ref), (v_hbm, v_ref), (w_hbm, w_ref), (x_hbm, x_ref),
                (rt_hbm, rt_ref), (u_hbm, u_ref), (r_hbm, r_ref),
            ]
        )
    ]
    for copy in copies:
        copy.start()
    err_ref[...] = jnp.zeros_like(err_ref)
    tag_err[...] = jnp.zeros_like(tag_err)
    for copy in copies[:4]:
        copy.wait()
    for s in range(x_ref.shape[0]):
        a, c = tile(xt_ref[0, s]), tile(xt_ref[1, s])
        e = dot_rows(v_ref[a, :], w_ref[c, :]) - x_ref[s].astype(F32)
        tag_err[a, c] = e.astype(BF16)
    for copy in copies[4:]:
        copy.wait()
    count = rc_ref[0]
    for s in range(r_ref.shape[0]):
        a, c = tile(rt_ref[0, s]), tile(rt_ref[1, s])
        e = dot_rows(u_ref[a, :], v_ref[c, :]) - r_ref[s].astype(F32)
        e = jnp.where(s < count, e, 0.0)
        err_ref[a, c] = e.astype(BF16)
    step = 256
    for i in range(0, item_ref.shape[0], step):
        rows = pl.ds(i, step)
        part = dot_cols(err_ref[:, rows], u_ref[...])
        part += jnp.dot(tag_err[rows, :], w_ref[...], preferred_element_type=F32)
        item_ref[rows, :] = part.astype(BF16)
    half = own_ref.shape[0]
    core = core_ref[0]
    mine, other = (pl.ds(pl.multiple_of(h * half, half), half) for h in (core, 1 - core))
    own_ref[...] = dot_cols(tag_err[:, mine], v_ref[...])
    part = dot_cols(tag_err[:, other], v_ref[...])
    send_ref[...] = part.astype(BF16)


def users_kernel(err_ref, u_ref, v_ref, out_ref):
    step = 256
    for i in range(0, out_ref.shape[0], step):
        rows = pl.ds(i, step)
        grad = jnp.dot(err_ref[rows, :], v_ref[...], preferred_element_type=F32)
        old = u_ref[rows, :].astype(F32)
        out_ref[rows, :] = (old - 0.04 * (grad + 0.05 * old)).astype(BF16)


def split_kernel(bit_ref, own_ref, arrived_ref, keep_ref, send_ref):
    size = keep_ref.shape[0]
    mine, other = (
        pl.ds(pl.multiple_of(h * size, size), size) for h in (bit_ref[0], 1 - bit_ref[0])
    )
    keep_ref[...] = own_ref[mine, :] + arrived_ref[mine, :].astype(F32)
    send_ref[...] = (own_ref[other, :] + arrived_ref[other, :].astype(F32)).astype(BF16)


def item_kernel(tag_ref, v_hbm, pieces_hbm, out_ref, old_ref, pieces_ref, sems):
    count, size = pieces_ref.shape[:2]
    group = count // 4
    start = pl.multiple_of(tag_ref[0] * size, size)
    copies = [
        pltpu.make_async_copy(
            pieces_hbm.at[pl.ds(g * group, group)], pieces_ref.at[pl.ds(g * group, group)], sems.at[g]
        )
        for g in range(4)
    ]
    copies.append(pltpu.make_async_copy(v_hbm.at[pl.ds(start, size)], old_ref, sems.at[4]))
    for copy in copies:
        copy.start()
    total = jnp.zeros(out_ref.shape, F32)
    for g in range(4):
        copies[g].wait()
        for k in range(g * group, (g + 1) * group):
            total += pieces_ref[k].astype(F32)
    copies[4].wait()
    old = old_ref[...].astype(F32)
    out_ref[...] = (old - 0.04 * (total + 0.05 * old)).astype(BF16)


def spread_kernel(shard_ref, out_hbm, sems):
    copies = [
        pltpu.make_async_copy(shard_ref, out_hbm.at[k], sems.at[k])
        for k in range(out_hbm.shape[0])
    ]
    for copy in copies:
        copy.start()
    for copy in copies:
        copy.wait()


def place_kernel(in_ref, out_ref, sems):
    copies = [
        pltpu.make_async_copy(in_ref.at[k], out_ref.at[k], sems.at[k])
        for k in range(out_ref.shape[0])
    ]
    for copy in copies:
        copy.start()
    for copy in copies:
        copy.wait()


def whole():
    return pl.BlockSpec(memory_space=pltpu.VMEM)


def scalars():
    return pl.BlockSpec(memory_space=pltpu.SMEM)


def in_hbm():
    return pl.BlockSpec(memory_space=pltpu.HBM)


def partials(rt, rc, xt, core, u, v, w, r, x):
    users, rank = u.shape
    items, tags = v.shape[0], w.shape[0]
    return pl.pallas_call(
        grads_kernel,
        out_shape=(
            jax.ShapeDtypeStruct((items, rank), BF16),
            jax.ShapeDtypeStruct((tags // 2, rank), BF16),
            jax.ShapeDtypeStruct((tags // 2, rank), F32),
            jax.ShapeDtypeStruct((users, items), BF16),
        ),
        in_specs=[scalars()] * 2 + [in_hbm()] * 7,
        out_specs=(whole(),) * 4,
        scratch_shapes=[pltpu.SMEM(a.shape, a.dtype) for a in (xt, rt)]
        + [pltpu.VMEM(a.shape, BF16) for a in (u, v, w, r, x)]
        + [
            pltpu.VMEM((items, tags), BF16),
            pltpu.SemaphoreType.DMA((7,)),
        ],
        compiler_params=pltpu.CompilerParams(vmem_limit_bytes=14 << 20),
        cost_estimate=pl.CostEstimate(flops=3 << 30, bytes_accessed=6 << 20, transcendentals=0),
    )(rc, core, *(pltpu.with_memory_space_constraint(a, pltpu.HBM) for a in (xt, rt, u, v, w, r, x)))


def updated_users(err, u, v):
    return pl.pallas_call(
        users_kernel,
        out_shape=jax.ShapeDtypeStruct(u.shape, BF16),
        in_specs=[whole()] * 3,
        out_specs=whole(),
        compiler_params=pltpu.CompilerParams(vmem_limit_bytes=6 << 20),
        cost_estimate=pl.CostEstimate(flops=1 << 30, bytes_accessed=4 << 20, transcendentals=0),
    )(err, u, v)


def split_sum(bit, own, arrived):
    size, rank = own.shape[0] // 2, own.shape[1]
    return pl.pallas_call(
        split_kernel,
        out_shape=(
            jax.ShapeDtypeStruct((size, rank), F32),
            jax.ShapeDtypeStruct((size, rank), BF16),
        ),
        in_specs=[scalars(), whole(), whole()],
        out_specs=(whole(),) * 2,
        compiler_params=pltpu.CompilerParams(vmem_limit_bytes=4 << 20),
        cost_estimate=pl.CostEstimate(flops=1 << 18, bytes_accessed=1 << 20, transcendentals=0),
    )(bit, own, arrived)


def updated_items(tag, v, pieces):
    count, size, rank = pieces.shape
    return pl.pallas_call(
        item_kernel,
        out_shape=jax.ShapeDtypeStruct((size, rank), BF16),
        in_specs=[scalars(), in_hbm(), in_hbm()],
        out_specs=whole(),
        scratch_shapes=[
            pltpu.VMEM((size, rank), BF16),
            pltpu.VMEM(pieces.shape, BF16),
            pltpu.SemaphoreType.DMA((5,)),
        ],
        compiler_params=pltpu.CompilerParams(vmem_limit_bytes=4 << 20),
        cost_estimate=pl.CostEstimate(flops=1 << 19, bytes_accessed=1 << 20, transcendentals=0),
    )(tag, *(pltpu.with_memory_space_constraint(a, pltpu.HBM) for a in (v, pieces)))


def spread(shard, count):
    return pl.pallas_call(
        spread_kernel,
        out_shape=jax.ShapeDtypeStruct((count,) + shard.shape, BF16),
        in_specs=[whole()],
        out_specs=in_hbm(),
        scratch_shapes=[pltpu.SemaphoreType.DMA((count,))],
        compiler_params=pltpu.CompilerParams(vmem_limit_bytes=2 << 20),
        cost_estimate=pl.CostEstimate(flops=0, bytes_accessed=1 << 20, transcendentals=0),
    )(shard)


def placed_items(pieces):
    return pl.pallas_call(
        place_kernel,
        out_shape=jax.ShapeDtypeStruct(pieces.shape, BF16),
        in_specs=[pl.BlockSpec(memory_space=pl.ANY)],
        out_specs=in_hbm(),
        scratch_shapes=[pltpu.SemaphoreType.DMA((pieces.shape[0],))],
        compiler_params=pltpu.CompilerParams(vmem_limit_bytes=2 << 20),
        cost_estimate=pl.CostEstimate(flops=0, bytes_accessed=2 << 20, transcendentals=0),
    )(pieces)


def exchanged(pieces, axis):
    return lax.all_to_all(pieces, axis, 0, 0)


def updated(old, total):
    old = old.astype(F32)
    return (old - 0.04 * (total + 0.05 * old)).astype(BF16)


def part_of(block, index, size):
    return lax.dynamic_slice_in_dim(block, index * size, size, 0)


def swapped(block, mask):
    n = lax.axis_size("rot")
    return lax.ppermute(block, "rot", [(i, i ^ mask) for i in range(n)])


def joined(mine, other, bit):
    return jnp.where(
        bit == 0, jnp.concatenate([mine, other], 0), jnp.concatenate([other, mine], 0)
    )


def added(own, mask):
    own = lax.reduce_precision(own, 8, 7)
    return own + swapped(own.astype(BF16), mask).astype(F32)


def tag_sum_nearby(send, own, y_bit):
    own, send = split_sum(y_bit[None], own, swapped(send, 1))
    return added(own + swapped(send, 4).astype(F32), 2)


def new_tag_rows(total, w, core, y_bit):
    shard = updated(part_of(w, core * 2 + y_bit, total.shape[0]), total)
    half = joined(shard, swapped(shard, 4), y_bit)
    return joined(half, swapped(half, 1), core)


def on_device(u, v, w, rating_tiles, rating_counts, ratings, tag_tiles, tag_values):
    rank = u.shape[1]
    n_rot, n_tag = lax.axis_size("rot"), lax.axis_size("tag")
    rot = lax.axis_index("rot")
    core, y_bit = rot & 1, (rot >> 2) & 1
    item_part, tag_send, tag_own, err = partials(
        rating_tiles.T, rating_counts, tag_tiles.T, core[None], u, v, w, ratings, tag_values
    )
    item_pieces = exchanged(item_part.reshape(n_tag, -1, rank), "tag")
    new_users = updated_users(err, u, v)
    tag_total = tag_sum_nearby(tag_send, tag_own, y_bit)
    item_pieces, _, _ = lax.optimization_barrier((item_pieces, tag_total, new_users))
    shard = updated_items(lax.axis_index("tag")[None], v, item_pieces)
    shard = lax.ppermute(shard, "rot", [(i, (i + 1) % n_rot) for i in range(n_rot)])
    tag_total = added(tag_total, 8)
    shard, _ = lax.optimization_barrier((shard, tag_total))
    rotated_items = placed_items(exchanged(spread(shard, n_tag), "tag")).reshape(v.shape)
    new_tags = new_tag_rows(added(tag_total, 16), w, core, y_bit)
    return (new_users, rotated_items, new_tags)


def solution(mesh):
    placed = (
        P(("rot", "tag"), None),
        P("rot", None),
        P("tag", None),
        P(("rot", "tag"), None),
        P(("rot", "tag")),
        P(("rot", "tag"), None, None),
        P(("rot", "tag"), None),
        P(("rot", "tag"), None, None),
    )
    return jax.shard_map(
        on_device,
        mesh=mesh,
        in_specs=placed,
        out_specs=(P(("rot", "tag"), None), P("rot", None), P("tag", None)),
        check_vma=False,
    )
```

```python
import jax
import jax.numpy as jnp
from jax import lax
from jax.experimental import pallas as pl
from jax.experimental.pallas import tpu as pltpu
from jax.sharding import PartitionSpec as P

TILE = 128
F32 = jnp.float32
BF16 = jnp.bfloat16


def tile(index):
    return pl.ds(pl.multiple_of(index * TILE, TILE), TILE)


def dot_rows(left, right):
    return lax.dot_general(left, right, (((1,), (1,)), ((), ())), preferred_element_type=F32)


def dot_cols(left, right):
    return lax.dot_general(left, right, (((0,), (0,)), ((), ())), preferred_element_type=F32)


def grads_kernel(
    rc_ref, core_ref, xt_hbm, rt_hbm, u_hbm, v_hbm, w_hbm, r_hbm, x_hbm,
    item_ref, send_ref, own_ref, err_ref,
    xt_ref, rt_ref, u_ref, v_ref, w_ref, r_ref, x_ref, tag_err, sems,
):
    copies = [
        pltpu.make_async_copy(src, dst, sems.at[i])
        for i, (src, dst) in enumerate(
            [
                (xt_hbm, xt_ref), (v_hbm, v_ref), (w_hbm, w_ref), (x_hbm, x_ref),
                (rt_hbm, rt_ref), (u_hbm, u_ref), (r_hbm, r_ref),
            ]
        )
    ]
    for copy in copies:
        copy.start()
    err_ref[...] = jnp.zeros_like(err_ref)
    tag_err[...] = jnp.zeros_like(tag_err)
    for copy in copies[:4]:
        copy.wait()
    for s in range(x_ref.shape[0]):
        a, c = tile(xt_ref[0, s]), tile(xt_ref[1, s])
        e = dot_rows(v_ref[a, :], w_ref[c, :]) - x_ref[s].astype(F32)
        tag_err[a, c] = e.astype(BF16)
    for copy in copies[4:]:
        copy.wait()
    count = rc_ref[0]
    for s in range(r_ref.shape[0]):
        a, c = tile(rt_ref[0, s]), tile(rt_ref[1, s])
        e = dot_rows(u_ref[a, :], v_ref[c, :]) - r_ref[s].astype(F32)
        e = jnp.where(s < count, e, 0.0)
        err_ref[a, c] = e.astype(BF16)
    step = 256
    for i in range(0, item_ref.shape[0], step):
        rows = pl.ds(i, step)
        part = dot_cols(err_ref[:, rows], u_ref[...])
        part += jnp.dot(tag_err[rows, :], w_ref[...], preferred_element_type=F32)
        item_ref[rows, :] = part.astype(BF16)
    half = own_ref.shape[0]
    core = core_ref[0]
    mine, other = (pl.ds(pl.multiple_of(h * half, half), half) for h in (core, 1 - core))
    own_ref[...] = dot_cols(tag_err[:, mine], v_ref[...])
    part = dot_cols(tag_err[:, other], v_ref[...])
    send_ref[...] = part.astype(BF16)


def users_kernel(err_ref, u_ref, v_ref, out_ref):
    step = 256
    for i in range(0, out_ref.shape[0], step):
        rows = pl.ds(i, step)
        grad = jnp.dot(err_ref[rows, :], v_ref[...], preferred_element_type=F32)
        old = u_ref[rows, :].astype(F32)
        out_ref[rows, :] = (old - 0.04 * (grad + 0.05 * old)).astype(BF16)


def split_kernel(bit_ref, own_ref, arrived_ref, keep_ref, send_ref):
    size = keep_ref.shape[0]
    mine, other = (
        pl.ds(pl.multiple_of(h * size, size), size) for h in (bit_ref[0], 1 - bit_ref[0])
    )
    keep_ref[...] = own_ref[mine, :] + arrived_ref[mine, :].astype(F32)
    send_ref[...] = (own_ref[other, :] + arrived_ref[other, :].astype(F32)).astype(BF16)


def item_kernel(tag_ref, v_hbm, pieces_hbm, out_ref, old_ref, pieces_ref, sems):
    count, size = pieces_ref.shape[:2]
    group = count // 4
    start = pl.multiple_of(tag_ref[0] * size, size)
    copies = [
        pltpu.make_async_copy(
            pieces_hbm.at[pl.ds(g * group, group)], pieces_ref.at[pl.ds(g * group, group)], sems.at[g]
        )
        for g in range(4)
    ]
    copies.append(pltpu.make_async_copy(v_hbm.at[pl.ds(start, size)], old_ref, sems.at[4]))
    for copy in copies:
        copy.start()
    total = jnp.zeros(out_ref.shape, F32)
    for g in range(4):
        copies[g].wait()
        for k in range(g * group, (g + 1) * group):
            total += pieces_ref[k].astype(F32)
    copies[4].wait()
    old = old_ref[...].astype(F32)
    out_ref[...] = (old - 0.04 * (total + 0.05 * old)).astype(BF16)


def spread_kernel(shard_ref, out_hbm, sems):
    copies = [
        pltpu.make_async_copy(shard_ref, out_hbm.at[k], sems.at[k])
        for k in range(out_hbm.shape[0])
    ]
    for copy in copies:
        copy.start()
    for copy in copies:
        copy.wait()


def place_kernel(in_ref, out_ref, sems):
    copies = [
        pltpu.make_async_copy(in_ref.at[k], out_ref.at[k], sems.at[k])
        for k in range(out_ref.shape[0])
    ]
    for copy in copies:
        copy.start()
    for copy in copies:
        copy.wait()


def whole():
    return pl.BlockSpec(memory_space=pltpu.VMEM)


def scalars():
    return pl.BlockSpec(memory_space=pltpu.SMEM)


def in_hbm():
    return pl.BlockSpec(memory_space=pltpu.HBM)


def partials(rt, rc, xt, core, u, v, w, r, x):
    users, rank = u.shape
    items, tags = v.shape[0], w.shape[0]
    return pl.pallas_call(
        grads_kernel,
        out_shape=(
            jax.ShapeDtypeStruct((items, rank), BF16),
            jax.ShapeDtypeStruct((tags // 2, rank), BF16),
            jax.ShapeDtypeStruct((tags // 2, rank), F32),
            jax.ShapeDtypeStruct((users, items), BF16),
        ),
        in_specs=[scalars()] * 2 + [in_hbm()] * 7,
        out_specs=(whole(),) * 4,
        scratch_shapes=[pltpu.SMEM(a.shape, a.dtype) for a in (xt, rt)]
        + [pltpu.VMEM(a.shape, BF16) for a in (u, v, w, r, x)]
        + [
            pltpu.VMEM((items, tags), BF16),
            pltpu.SemaphoreType.DMA((7,)),
        ],
        compiler_params=pltpu.CompilerParams(vmem_limit_bytes=14 << 20),
        cost_estimate=pl.CostEstimate(flops=3 << 30, bytes_accessed=6 << 20, transcendentals=0),
    )(rc, core, *(pltpu.with_memory_space_constraint(a, pltpu.HBM) for a in (xt, rt, u, v, w, r, x)))


def updated_users(err, u, v):
    return pl.pallas_call(
        users_kernel,
        out_shape=jax.ShapeDtypeStruct(u.shape, BF16),
        in_specs=[whole()] * 3,
        out_specs=whole(),
        compiler_params=pltpu.CompilerParams(vmem_limit_bytes=6 << 20),
        cost_estimate=pl.CostEstimate(flops=1 << 30, bytes_accessed=4 << 20, transcendentals=0),
    )(err, u, v)


def split_sum(bit, own, arrived):
    size, rank = own.shape[0] // 2, own.shape[1]
    return pl.pallas_call(
        split_kernel,
        out_shape=(
            jax.ShapeDtypeStruct((size, rank), F32),
            jax.ShapeDtypeStruct((size, rank), BF16),
        ),
        in_specs=[scalars(), whole(), whole()],
        out_specs=(whole(),) * 2,
        compiler_params=pltpu.CompilerParams(vmem_limit_bytes=4 << 20),
        cost_estimate=pl.CostEstimate(flops=1 << 18, bytes_accessed=1 << 20, transcendentals=0),
    )(bit, own, arrived)


def updated_items(tag, v, pieces):
    count, size, rank = pieces.shape
    return pl.pallas_call(
        item_kernel,
        out_shape=jax.ShapeDtypeStruct((size, rank), BF16),
        in_specs=[scalars(), in_hbm(), in_hbm()],
        out_specs=whole(),
        scratch_shapes=[
            pltpu.VMEM((size, rank), BF16),
            pltpu.VMEM(pieces.shape, BF16),
            pltpu.SemaphoreType.DMA((5,)),
        ],
        compiler_params=pltpu.CompilerParams(vmem_limit_bytes=4 << 20),
        cost_estimate=pl.CostEstimate(flops=1 << 19, bytes_accessed=1 << 20, transcendentals=0),
    )(tag, *(pltpu.with_memory_space_constraint(a, pltpu.HBM) for a in (v, pieces)))


def spread(shard, count):
    return pl.pallas_call(
        spread_kernel,
        out_shape=jax.ShapeDtypeStruct((count,) + shard.shape, BF16),
        in_specs=[whole()],
        out_specs=in_hbm(),
        scratch_shapes=[pltpu.SemaphoreType.DMA((count,))],
        compiler_params=pltpu.CompilerParams(vmem_limit_bytes=2 << 20),
        cost_estimate=pl.CostEstimate(flops=0, bytes_accessed=1 << 20, transcendentals=0),
    )(shard)


def placed_items(pieces):
    return pl.pallas_call(
        place_kernel,
        out_shape=jax.ShapeDtypeStruct(pieces.shape, BF16),
        in_specs=[pl.BlockSpec(memory_space=pl.ANY)],
        out_specs=in_hbm(),
        scratch_shapes=[pltpu.SemaphoreType.DMA((pieces.shape[0],))],
        compiler_params=pltpu.CompilerParams(vmem_limit_bytes=2 << 20),
        cost_estimate=pl.CostEstimate(flops=0, bytes_accessed=2 << 20, transcendentals=0),
    )(pieces)


def exchanged(pieces, axis):
    return lax.all_to_all(pieces, axis, 0, 0)


def updated(old, total):
    old = old.astype(F32)
    return (old - 0.04 * (total + 0.05 * old)).astype(BF16)


def part_of(block, index, size):
    return lax.dynamic_slice_in_dim(block, index * size, size, 0)


def swapped(block, mask):
    n = lax.axis_size("rot")
    return lax.ppermute(block, "rot", [(i, i ^ mask) for i in range(n)])


def joined(mine, other, bit):
    return jnp.where(
        bit == 0, jnp.concatenate([mine, other], 0), jnp.concatenate([other, mine], 0)
    )


def added(own, mask):
    own = lax.reduce_precision(own, 8, 7)
    return own + swapped(own.astype(BF16), mask).astype(F32)


def tag_sum_nearby(send, own, y_bit):
    own, send = split_sum(y_bit[None], own, swapped(send, 1))
    return added(own + swapped(send, 4).astype(F32), 8)


def new_tag_rows(total, w, core, y_bit):
    shard = updated(part_of(w, core * 2 + y_bit, total.shape[0]), total)
    half = joined(shard, swapped(shard, 4), y_bit)
    return joined(half, swapped(half, 1), core)


def on_device(u, v, w, rating_tiles, rating_counts, ratings, tag_tiles, tag_values):
    rank = u.shape[1]
    n_rot, n_tag = lax.axis_size("rot"), lax.axis_size("tag")
    rot = lax.axis_index("rot")
    core, y_bit = rot & 1, (rot >> 2) & 1
    item_part, tag_send, tag_own, err = partials(
        rating_tiles.T, rating_counts, tag_tiles.T, core[None], u, v, w, ratings, tag_values
    )
    item_pieces = exchanged(item_part.reshape(n_tag, -1, rank), "tag")
    new_users = updated_users(err, u, v)
    tag_total = tag_sum_nearby(tag_send, tag_own, y_bit)
    item_pieces, _, _ = lax.optimization_barrier((item_pieces, tag_total, new_users))
    shard = updated_items(lax.axis_index("tag")[None], v, item_pieces)
    shard = lax.ppermute(shard, "rot", [(i, (i + 1) % n_rot) for i in range(n_rot)])
    tag_total = added(tag_total, 2)
    shard, _ = lax.optimization_barrier((shard, tag_total))
    rotated_items = placed_items(exchanged(spread(shard, n_tag), "tag")).reshape(v.shape)
    new_tags = new_tag_rows(added(tag_total, 16), w, core, y_bit)
    return (new_users, rotated_items, new_tags)


def solution(mesh):
    placed = (
        P(("rot", "tag"), None),
        P("rot", None),
        P("tag", None),
        P(("rot", "tag"), None),
        P(("rot", "tag")),
        P(("rot", "tag"), None, None),
        P(("rot", "tag"), None),
        P(("rot", "tag"), None, None),
    )
    return jax.shard_map(
        on_device,
        mesh=mesh,
        in_specs=placed,
        out_specs=(P(("rot", "tag"), None), P("rot", None), P("tag", None)),
        check_vma=False,
    )
```

```python
import jax
import jax.numpy as jnp
from jax import lax
from jax.experimental import pallas as pl
from jax.experimental.pallas import tpu as pltpu
from jax.sharding import PartitionSpec as P

TILE = 128
F32 = jnp.float32
BF16 = jnp.bfloat16


def tile(index):
    return pl.ds(pl.multiple_of(index * TILE, TILE), TILE)


def dot_rows(left, right):
    return lax.dot_general(left, right, (((1,), (1,)), ((), ())), preferred_element_type=F32)


def dot_cols(left, right):
    return lax.dot_general(left, right, (((0,), (0,)), ((), ())), preferred_element_type=F32)


def grads_kernel(
    rc_ref, core_ref, xt_hbm, rt_hbm, u_hbm, v_hbm, w_hbm, r_hbm, x_hbm,
    item_ref, send_ref, own_ref, err_ref,
    xt_ref, rt_ref, u_ref, v_ref, w_ref, r_ref, x_ref, tag_err, sems,
):
    copies = [
        pltpu.make_async_copy(src, dst, sems.at[i])
        for i, (src, dst) in enumerate(
            [
                (xt_hbm, xt_ref), (v_hbm, v_ref), (w_hbm, w_ref), (x_hbm, x_ref),
                (rt_hbm, rt_ref), (u_hbm, u_ref), (r_hbm, r_ref),
            ]
        )
    ]
    for copy in copies:
        copy.start()
    err_ref[...] = jnp.zeros_like(err_ref)
    tag_err[...] = jnp.zeros_like(tag_err)
    for copy in copies[:4]:
        copy.wait()
    for s in range(x_ref.shape[0]):
        a, c = tile(xt_ref[0, s]), tile(xt_ref[1, s])
        e = dot_rows(v_ref[a, :], w_ref[c, :]) - x_ref[s].astype(F32)
        tag_err[a, c] = e.astype(BF16)
    for copy in copies[4:]:
        copy.wait()
    count = rc_ref[0]
    for s in range(r_ref.shape[0]):
        a, c = tile(rt_ref[0, s]), tile(rt_ref[1, s])
        e = dot_rows(u_ref[a, :], v_ref[c, :]) - r_ref[s].astype(F32)
        e = jnp.where(s < count, e, 0.0)
        err_ref[a, c] = e.astype(BF16)
    step = 256
    for i in range(0, item_ref.shape[0], step):
        rows = pl.ds(i, step)
        part = dot_cols(err_ref[:, rows], u_ref[...])
        part += jnp.dot(tag_err[rows, :], w_ref[...], preferred_element_type=F32)
        item_ref[rows, :] = part.astype(BF16)
    half = own_ref.shape[0]
    core = core_ref[0]
    mine, other = (pl.ds(pl.multiple_of(h * half, half), half) for h in (core, 1 - core))
    own_ref[...] = dot_cols(tag_err[:, mine], v_ref[...])
    part = dot_cols(tag_err[:, other], v_ref[...])
    send_ref[...] = part.astype(BF16)


def users_kernel(err_ref, u_ref, v_ref, out_ref):
    step = 256
    for i in range(0, out_ref.shape[0], step):
        rows = pl.ds(i, step)
        grad = jnp.dot(err_ref[rows, :], v_ref[...], preferred_element_type=F32)
        old = u_ref[rows, :].astype(F32)
        out_ref[rows, :] = (old - 0.04 * (grad + 0.05 * old)).astype(BF16)


def split_kernel(bit_ref, own_ref, arrived_ref, keep_ref, send_ref):
    size = keep_ref.shape[0]
    mine, other = (
        pl.ds(pl.multiple_of(h * size, size), size) for h in (bit_ref[0], 1 - bit_ref[0])
    )
    keep_ref[...] = own_ref[mine, :] + arrived_ref[mine, :].astype(F32)
    send_ref[...] = (own_ref[other, :] + arrived_ref[other, :].astype(F32)).astype(BF16)


def item_kernel(tag_ref, v_hbm, pieces_hbm, out_ref, old_ref, pieces_ref, sems):
    count, size = pieces_ref.shape[:2]
    group = count // 4
    start = pl.multiple_of(tag_ref[0] * size, size)
    copies = [
        pltpu.make_async_copy(
            pieces_hbm.at[pl.ds(g * group, group)], pieces_ref.at[pl.ds(g * group, group)], sems.at[g]
        )
        for g in range(4)
    ]
    copies.append(pltpu.make_async_copy(v_hbm.at[pl.ds(start, size)], old_ref, sems.at[4]))
    for copy in copies:
        copy.start()
    total = jnp.zeros(out_ref.shape, F32)
    for g in range(4):
        copies[g].wait()
        for k in range(g * group, (g + 1) * group):
            total += pieces_ref[k].astype(F32)
    copies[4].wait()
    old = old_ref[...].astype(F32)
    out_ref[...] = (old - 0.04 * (total + 0.05 * old)).astype(BF16)


def spread_kernel(shard_ref, out_hbm, sems):
    copies = [
        pltpu.make_async_copy(shard_ref, out_hbm.at[k], sems.at[k])
        for k in range(out_hbm.shape[0])
    ]
    for copy in copies:
        copy.start()
    for copy in copies:
        copy.wait()


def place_kernel(in_ref, out_ref, sems):
    copies = [
        pltpu.make_async_copy(in_ref.at[k], out_ref.at[k], sems.at[k])
        for k in range(out_ref.shape[0])
    ]
    for copy in copies:
        copy.start()
    for copy in copies:
        copy.wait()


def whole():
    return pl.BlockSpec(memory_space=pltpu.VMEM)


def scalars():
    return pl.BlockSpec(memory_space=pltpu.SMEM)


def in_hbm():
    return pl.BlockSpec(memory_space=pltpu.HBM)


def partials(rt, rc, xt, core, u, v, w, r, x):
    users, rank = u.shape
    items, tags = v.shape[0], w.shape[0]
    return pl.pallas_call(
        grads_kernel,
        out_shape=(
            jax.ShapeDtypeStruct((items, rank), BF16),
            jax.ShapeDtypeStruct((tags // 2, rank), BF16),
            jax.ShapeDtypeStruct((tags // 2, rank), F32),
            jax.ShapeDtypeStruct((users, items), BF16),
        ),
        in_specs=[scalars()] * 2 + [in_hbm()] * 7,
        out_specs=(whole(),) * 4,
        scratch_shapes=[pltpu.SMEM(a.shape, a.dtype) for a in (xt, rt)]
        + [pltpu.VMEM(a.shape, BF16) for a in (u, v, w, r, x)]
        + [
            pltpu.VMEM((items, tags), BF16),
            pltpu.SemaphoreType.DMA((7,)),
        ],
        compiler_params=pltpu.CompilerParams(vmem_limit_bytes=14 << 20),
        cost_estimate=pl.CostEstimate(flops=3 << 30, bytes_accessed=6 << 20, transcendentals=0),
    )(rc, core, *(pltpu.with_memory_space_constraint(a, pltpu.HBM) for a in (xt, rt, u, v, w, r, x)))


def updated_users(err, u, v):
    return pl.pallas_call(
        users_kernel,
        out_shape=jax.ShapeDtypeStruct(u.shape, BF16),
        in_specs=[whole()] * 3,
        out_specs=whole(),
        compiler_params=pltpu.CompilerParams(vmem_limit_bytes=6 << 20),
        cost_estimate=pl.CostEstimate(flops=1 << 30, bytes_accessed=4 << 20, transcendentals=0),
    )(err, u, v)


def split_sum(bit, own, arrived):
    size, rank = own.shape[0] // 2, own.shape[1]
    return pl.pallas_call(
        split_kernel,
        out_shape=(
            jax.ShapeDtypeStruct((size, rank), F32),
            jax.ShapeDtypeStruct((size, rank), BF16),
        ),
        in_specs=[scalars(), whole(), whole()],
        out_specs=(whole(),) * 2,
        compiler_params=pltpu.CompilerParams(vmem_limit_bytes=4 << 20),
        cost_estimate=pl.CostEstimate(flops=1 << 18, bytes_accessed=1 << 20, transcendentals=0),
    )(bit, own, arrived)


def updated_items(tag, v, pieces):
    count, size, rank = pieces.shape
    return pl.pallas_call(
        item_kernel,
        out_shape=jax.ShapeDtypeStruct((size, rank), BF16),
        in_specs=[scalars(), in_hbm(), in_hbm()],
        out_specs=whole(),
        scratch_shapes=[
            pltpu.VMEM((size, rank), BF16),
            pltpu.VMEM(pieces.shape, BF16),
            pltpu.SemaphoreType.DMA((5,)),
        ],
        compiler_params=pltpu.CompilerParams(vmem_limit_bytes=4 << 20),
        cost_estimate=pl.CostEstimate(flops=1 << 19, bytes_accessed=1 << 20, transcendentals=0),
    )(tag, *(pltpu.with_memory_space_constraint(a, pltpu.HBM) for a in (v, pieces)))


def spread(shard, count):
    return pl.pallas_call(
        spread_kernel,
        out_shape=jax.ShapeDtypeStruct((count,) + shard.shape, BF16),
        in_specs=[whole()],
        out_specs=in_hbm(),
        scratch_shapes=[pltpu.SemaphoreType.DMA((count,))],
        compiler_params=pltpu.CompilerParams(vmem_limit_bytes=2 << 20),
        cost_estimate=pl.CostEstimate(flops=0, bytes_accessed=1 << 20, transcendentals=0),
    )(shard)


def placed_items(pieces):
    return pl.pallas_call(
        place_kernel,
        out_shape=jax.ShapeDtypeStruct(pieces.shape, BF16),
        in_specs=[pl.BlockSpec(memory_space=pl.ANY)],
        out_specs=in_hbm(),
        scratch_shapes=[pltpu.SemaphoreType.DMA((pieces.shape[0],))],
        compiler_params=pltpu.CompilerParams(vmem_limit_bytes=2 << 20),
        cost_estimate=pl.CostEstimate(flops=0, bytes_accessed=2 << 20, transcendentals=0),
    )(pieces)


def exchanged(pieces, axis):
    return lax.all_to_all(pieces, axis, 0, 0)


def updated(old, total):
    old = old.astype(F32)
    return (old - 0.04 * (total + 0.05 * old)).astype(BF16)


def part_of(block, index, size):
    return lax.dynamic_slice_in_dim(block, index * size, size, 0)


def swapped(block, mask):
    n = lax.axis_size("rot")
    return lax.ppermute(block, "rot", [(i, i ^ mask) for i in range(n)])


def joined(mine, other, bit):
    return jnp.where(
        bit == 0, jnp.concatenate([mine, other], 0), jnp.concatenate([other, mine], 0)
    )


def added(own, mask):
    own = lax.reduce_precision(own, 8, 7)
    return own + swapped(own.astype(BF16), mask).astype(F32)


def tag_sum_nearby(send, own, y_bit):
    own, send = split_sum(y_bit[None], own, swapped(send, 1))
    return added(own + swapped(send, 4).astype(F32), 16)


def new_tag_rows(total, w, core, y_bit):
    shard = updated(part_of(w, core * 2 + y_bit, total.shape[0]), total)
    half = joined(shard, swapped(shard, 4), y_bit)
    return joined(half, swapped(half, 1), core)


def on_device(u, v, w, rating_tiles, rating_counts, ratings, tag_tiles, tag_values):
    rank = u.shape[1]
    n_rot, n_tag = lax.axis_size("rot"), lax.axis_size("tag")
    rot = lax.axis_index("rot")
    core, y_bit = rot & 1, (rot >> 2) & 1
    item_part, tag_send, tag_own, err = partials(
        rating_tiles.T, rating_counts, tag_tiles.T, core[None], u, v, w, ratings, tag_values
    )
    item_pieces = exchanged(item_part.reshape(n_tag, -1, rank), "tag")
    new_users = updated_users(err, u, v)
    tag_total = tag_sum_nearby(tag_send, tag_own, y_bit)
    item_pieces, _, _ = lax.optimization_barrier((item_pieces, tag_total, new_users))
    shard = updated_items(lax.axis_index("tag")[None], v, item_pieces)
    shard = lax.ppermute(shard, "rot", [(i, (i + 1) % n_rot) for i in range(n_rot)])
    tag_total = added(tag_total, 2)
    shard, _ = lax.optimization_barrier((shard, tag_total))
    rotated_items = placed_items(exchanged(spread(shard, n_tag), "tag")).reshape(v.shape)
    new_tags = new_tag_rows(added(tag_total, 8), w, core, y_bit)
    return (new_users, rotated_items, new_tags)


def solution(mesh):
    placed = (
        P(("rot", "tag"), None),
        P("rot", None),
        P("tag", None),
        P(("rot", "tag"), None),
        P(("rot", "tag")),
        P(("rot", "tag"), None, None),
        P(("rot", "tag"), None),
        P(("rot", "tag"), None, None),
    )
    return jax.shard_map(
        on_device,
        mesh=mesh,
        in_specs=placed,
        out_specs=(P(("rot", "tag"), None), P("rot", None), P("tag", None)),
        check_vma=False,
    )
```

```python
import jax
import jax.numpy as jnp
from jax import lax
from jax.experimental import pallas as pl
from jax.experimental.pallas import tpu as pltpu
from jax.sharding import PartitionSpec as P

TILE = 128
F32 = jnp.float32
BF16 = jnp.bfloat16


def tile(index):
    return pl.ds(pl.multiple_of(index * TILE, TILE), TILE)


def dot_rows(left, right):
    return lax.dot_general(left, right, (((1,), (1,)), ((), ())), preferred_element_type=F32)


def dot_cols(left, right):
    return lax.dot_general(left, right, (((0,), (0,)), ((), ())), preferred_element_type=F32)


def grads_kernel(
    rc_ref, core_ref, xt_hbm, rt_hbm, u_hbm, v_hbm, w_hbm, r_hbm, x_hbm,
    item_hbm, send_ref, own_ref, err_ref,
    xt_ref, rt_ref, u_ref, v_ref, w_ref, r_ref, x_ref, tag_err, item_ref, sems, out_sems,
):
    copies = [
        pltpu.make_async_copy(src, dst, sems.at[i])
        for i, (src, dst) in enumerate(
            [
                (xt_hbm, xt_ref), (v_hbm, v_ref), (w_hbm, w_ref), (x_hbm, x_ref),
                (rt_hbm, rt_ref), (u_hbm, u_ref), (r_hbm, r_ref),
            ]
        )
    ]
    for copy in copies:
        copy.start()
    err_ref[...] = jnp.zeros_like(err_ref)
    tag_err[...] = jnp.zeros_like(tag_err)
    for copy in copies[:4]:
        copy.wait()
    for s in range(x_ref.shape[0]):
        a, c = tile(xt_ref[0, s]), tile(xt_ref[1, s])
        e = dot_rows(v_ref[a, :], w_ref[c, :]) - x_ref[s].astype(F32)
        tag_err[a, c] = e.astype(BF16)
    for copy in copies[4:]:
        copy.wait()
    count = rc_ref[0]
    for s in range(r_ref.shape[0]):
        a, c = tile(rt_ref[0, s]), tile(rt_ref[1, s])
        e = dot_rows(u_ref[a, :], v_ref[c, :]) - r_ref[s].astype(F32)
        e = jnp.where(s < count, e, 0.0)
        err_ref[a, c] = e.astype(BF16)
    step = 256
    leaving = []
    for i in range(0, item_ref.shape[0], step):
        rows = pl.ds(i, step)
        part = dot_cols(err_ref[:, rows], u_ref[...])
        part += jnp.dot(tag_err[rows, :], w_ref[...], preferred_element_type=F32)
        item_ref[rows, :] = part.astype(BF16)
        leaving.append(
            pltpu.make_async_copy(item_ref.at[rows], item_hbm.at[rows], out_sems.at[i // step])
        )
        leaving[-1].start()
    half = own_ref.shape[0]
    core = core_ref[0]
    mine, other = (pl.ds(pl.multiple_of(h * half, half), half) for h in (core, 1 - core))
    own_ref[...] = dot_cols(tag_err[:, mine], v_ref[...])
    part = dot_cols(tag_err[:, other], v_ref[...])
    send_ref[...] = part.astype(BF16)
    for copy in leaving:
        copy.wait()


def users_kernel(err_ref, u_ref, v_ref, out_ref):
    step = 256
    for i in range(0, out_ref.shape[0], step):
        rows = pl.ds(i, step)
        grad = jnp.dot(err_ref[rows, :], v_ref[...], preferred_element_type=F32)
        old = u_ref[rows, :].astype(F32)
        out_ref[rows, :] = (old - 0.04 * (grad + 0.05 * old)).astype(BF16)


def split_kernel(bit_ref, own_ref, arrived_ref, keep_ref, send_ref):
    size = keep_ref.shape[0]
    mine, other = (
        pl.ds(pl.multiple_of(h * size, size), size) for h in (bit_ref[0], 1 - bit_ref[0])
    )
    keep_ref[...] = own_ref[mine, :] + arrived_ref[mine, :].astype(F32)
    send_ref[...] = (own_ref[other, :] + arrived_ref[other, :].astype(F32)).astype(BF16)


def item_kernel(tag_ref, v_hbm, pieces_hbm, out_ref, old_ref, pieces_ref, sems):
    count, size = pieces_ref.shape[:2]
    group = count // 4
    start = pl.multiple_of(tag_ref[0] * size, size)
    copies = [
        pltpu.make_async_copy(
            pieces_hbm.at[pl.ds(g * group, group)], pieces_ref.at[pl.ds(g * group, group)], sems.at[g]
        )
        for g in range(4)
    ]
    copies.append(pltpu.make_async_copy(v_hbm.at[pl.ds(start, size)], old_ref, sems.at[4]))
    for copy in copies:
        copy.start()
    total = jnp.zeros(out_ref.shape, F32)
    for g in range(4):
        copies[g].wait()
        for k in range(g * group, (g + 1) * group):
            total += pieces_ref[k].astype(F32)
    copies[4].wait()
    old = old_ref[...].astype(F32)
    out_ref[...] = (old - 0.04 * (total + 0.05 * old)).astype(BF16)


def spread_kernel(shard_ref, out_hbm, sems):
    copies = [
        pltpu.make_async_copy(shard_ref, out_hbm.at[k], sems.at[k])
        for k in range(out_hbm.shape[0])
    ]
    for copy in copies:
        copy.start()
    for copy in copies:
        copy.wait()


def place_kernel(in_ref, out_ref, sems):
    copies = [
        pltpu.make_async_copy(in_ref.at[k], out_ref.at[k], sems.at[k])
        for k in range(out_ref.shape[0])
    ]
    for copy in copies:
        copy.start()
    for copy in copies:
        copy.wait()


def whole():
    return pl.BlockSpec(memory_space=pltpu.VMEM)


def scalars():
    return pl.BlockSpec(memory_space=pltpu.SMEM)


def in_hbm():
    return pl.BlockSpec(memory_space=pltpu.HBM)


def partials(rt, rc, xt, core, u, v, w, r, x):
    users, rank = u.shape
    items, tags = v.shape[0], w.shape[0]
    return pl.pallas_call(
        grads_kernel,
        out_shape=(
            jax.ShapeDtypeStruct((items, rank), BF16),
            jax.ShapeDtypeStruct((tags // 2, rank), BF16),
            jax.ShapeDtypeStruct((tags // 2, rank), F32),
            jax.ShapeDtypeStruct((users, items), BF16),
        ),
        in_specs=[scalars()] * 2 + [in_hbm()] * 7,
        out_specs=(in_hbm(),) + (whole(),) * 3,
        scratch_shapes=[pltpu.SMEM(a.shape, a.dtype) for a in (xt, rt)]
        + [pltpu.VMEM(a.shape, BF16) for a in (u, v, w, r, x)]
        + [
            pltpu.VMEM((items, tags), BF16),
            pltpu.VMEM((items, rank), BF16),
            pltpu.SemaphoreType.DMA((7,)),
            pltpu.SemaphoreType.DMA((items // 256,)),
        ],
        compiler_params=pltpu.CompilerParams(vmem_limit_bytes=14 << 20),
        cost_estimate=pl.CostEstimate(flops=3 << 30, bytes_accessed=6 << 20, transcendentals=0),
    )(rc, core, *(pltpu.with_memory_space_constraint(a, pltpu.HBM) for a in (xt, rt, u, v, w, r, x)))


def updated_users(err, u, v):
    return pl.pallas_call(
        users_kernel,
        out_shape=jax.ShapeDtypeStruct(u.shape, BF16),
        in_specs=[whole()] * 3,
        out_specs=whole(),
        compiler_params=pltpu.CompilerParams(vmem_limit_bytes=6 << 20),
        cost_estimate=pl.CostEstimate(flops=1 << 30, bytes_accessed=4 << 20, transcendentals=0),
    )(err, u, v)


def split_sum(bit, own, arrived):
    size, rank = own.shape[0] // 2, own.shape[1]
    return pl.pallas_call(
        split_kernel,
        out_shape=(
            jax.ShapeDtypeStruct((size, rank), F32),
            jax.ShapeDtypeStruct((size, rank), BF16),
        ),
        in_specs=[scalars(), whole(), whole()],
        out_specs=(whole(),) * 2,
        compiler_params=pltpu.CompilerParams(vmem_limit_bytes=4 << 20),
        cost_estimate=pl.CostEstimate(flops=1 << 18, bytes_accessed=1 << 20, transcendentals=0),
    )(bit, own, arrived)


def updated_items(tag, v, pieces):
    count, size, rank = pieces.shape
    return pl.pallas_call(
        item_kernel,
        out_shape=jax.ShapeDtypeStruct((size, rank), BF16),
        in_specs=[scalars(), in_hbm(), in_hbm()],
        out_specs=whole(),
        scratch_shapes=[
            pltpu.VMEM((size, rank), BF16),
            pltpu.VMEM(pieces.shape, BF16),
            pltpu.SemaphoreType.DMA((5,)),
        ],
        compiler_params=pltpu.CompilerParams(vmem_limit_bytes=4 << 20),
        cost_estimate=pl.CostEstimate(flops=1 << 19, bytes_accessed=1 << 20, transcendentals=0),
    )(tag, *(pltpu.with_memory_space_constraint(a, pltpu.HBM) for a in (v, pieces)))


def spread(shard, count):
    return pl.pallas_call(
        spread_kernel,
        out_shape=jax.ShapeDtypeStruct((count,) + shard.shape, BF16),
        in_specs=[whole()],
        out_specs=in_hbm(),
        scratch_shapes=[pltpu.SemaphoreType.DMA((count,))],
        compiler_params=pltpu.CompilerParams(vmem_limit_bytes=2 << 20),
        cost_estimate=pl.CostEstimate(flops=0, bytes_accessed=1 << 20, transcendentals=0),
    )(shard)


def placed_items(pieces):
    return pl.pallas_call(
        place_kernel,
        out_shape=jax.ShapeDtypeStruct(pieces.shape, BF16),
        in_specs=[pl.BlockSpec(memory_space=pl.ANY)],
        out_specs=in_hbm(),
        scratch_shapes=[pltpu.SemaphoreType.DMA((pieces.shape[0],))],
        compiler_params=pltpu.CompilerParams(vmem_limit_bytes=2 << 20),
        cost_estimate=pl.CostEstimate(flops=0, bytes_accessed=2 << 20, transcendentals=0),
    )(pieces)


def exchanged(pieces, axis):
    return lax.all_to_all(pieces, axis, 0, 0)


def updated(old, total):
    old = old.astype(F32)
    return (old - 0.04 * (total + 0.05 * old)).astype(BF16)


def part_of(block, index, size):
    return lax.dynamic_slice_in_dim(block, index * size, size, 0)


def swapped(block, mask):
    n = lax.axis_size("rot")
    return lax.ppermute(block, "rot", [(i, i ^ mask) for i in range(n)])


def joined(mine, other, bit):
    return jnp.where(
        bit == 0, jnp.concatenate([mine, other], 0), jnp.concatenate([other, mine], 0)
    )


def added(own, mask):
    own = lax.reduce_precision(own, 8, 7)
    return own + swapped(own.astype(BF16), mask).astype(F32)


def tag_sum_nearby(send, own, y_bit):
    own, send = split_sum(y_bit[None], own, swapped(send, 1))
    return added(own + swapped(send, 4).astype(F32), 8)


def new_tag_rows(total, w, core, y_bit):
    shard = updated(part_of(w, core * 2 + y_bit, total.shape[0]), total)
    half = joined(shard, swapped(shard, 4), y_bit)
    return joined(half, swapped(half, 1), core)


def on_device(u, v, w, rating_tiles, rating_counts, ratings, tag_tiles, tag_values):
    rank = u.shape[1]
    n_rot, n_tag = lax.axis_size("rot"), lax.axis_size("tag")
    rot = lax.axis_index("rot")
    core, y_bit = rot & 1, (rot >> 2) & 1
    item_part, tag_send, tag_own, err = partials(
        rating_tiles.T, rating_counts, tag_tiles.T, core[None], u, v, w, ratings, tag_values
    )
    item_pieces = exchanged(item_part.reshape(n_tag, -1, rank), "tag")
    new_users = updated_users(err, u, v)
    tag_total = tag_sum_nearby(tag_send, tag_own, y_bit)
    item_pieces, _, _ = lax.optimization_barrier((item_pieces, tag_total, new_users))
    shard = updated_items(lax.axis_index("tag")[None], v, item_pieces)
    shard = lax.ppermute(shard, "rot", [(i, (i + 1) % n_rot) for i in range(n_rot)])
    tag_total = added(tag_total, 2)
    shard, _ = lax.optimization_barrier((shard, tag_total))
    rotated_items = placed_items(exchanged(spread(shard, n_tag), "tag")).reshape(v.shape)
    new_tags = new_tag_rows(added(tag_total, 16), w, core, y_bit)
    return (new_users, rotated_items, new_tags)


def solution(mesh):
    placed = (
        P(("rot", "tag"), None),
        P("rot", None),
        P("tag", None),
        P(("rot", "tag"), None),
        P(("rot", "tag")),
        P(("rot", "tag"), None, None),
        P(("rot", "tag"), None),
        P(("rot", "tag"), None, None),
    )
    return jax.shard_map(
        on_device,
        mesh=mesh,
        in_specs=placed,
        out_specs=(P(("rot", "tag"), None), P("rot", None), P("tag", None)),
        check_vma=False,
    )
```

```python
import jax
import jax.numpy as jnp
from jax import lax
from jax.experimental import pallas as pl
from jax.experimental.pallas import tpu as pltpu
from jax.sharding import PartitionSpec as P

TILE = 128
F32 = jnp.float32
BF16 = jnp.bfloat16


def tile(index):
    return pl.ds(pl.multiple_of(index * TILE, TILE), TILE)


def dot_rows(left, right):
    return lax.dot_general(left, right, (((1,), (1,)), ((), ())), preferred_element_type=F32)


def dot_cols(left, right):
    return lax.dot_general(left, right, (((0,), (0,)), ((), ())), preferred_element_type=F32)


def grads_kernel(
    rc_ref, core_ref, xt_hbm, rt_hbm, u_hbm, v_hbm, w_hbm, r_hbm, x_hbm,
    item_hbm, send_ref, own_ref, err_ref,
    xt_ref, rt_ref, u_ref, v_ref, w_ref, r_ref, x_ref, tag_err, item_ref, sems, out_sems,
):
    copies = [
        pltpu.make_async_copy(src, dst, sems.at[i])
        for i, (src, dst) in enumerate(
            [
                (xt_hbm, xt_ref), (v_hbm, v_ref), (w_hbm, w_ref), (x_hbm, x_ref),
                (rt_hbm, rt_ref), (u_hbm, u_ref), (r_hbm, r_ref),
            ]
        )
    ]
    for copy in copies:
        copy.start()
    err_ref[...] = jnp.zeros_like(err_ref)
    tag_err[...] = jnp.zeros_like(tag_err)
    for copy in copies[:4]:
        copy.wait()
    for s in range(x_ref.shape[0]):
        a, c = tile(xt_ref[0, s]), tile(xt_ref[1, s])
        e = dot_rows(v_ref[a, :], w_ref[c, :]) - x_ref[s].astype(F32)
        tag_err[a, c] = e.astype(BF16)
    for copy in copies[4:]:
        copy.wait()
    count = rc_ref[0]
    for s in range(r_ref.shape[0]):
        a, c = tile(rt_ref[0, s]), tile(rt_ref[1, s])
        e = dot_rows(u_ref[a, :], v_ref[c, :]) - r_ref[s].astype(F32)
        e = jnp.where(s < count, e, 0.0)
        err_ref[a, c] = e.astype(BF16)
    step = 256
    leaving = []
    for i in range(0, item_ref.shape[0], step):
        rows = pl.ds(i, step)
        part = dot_cols(err_ref[:, rows], u_ref[...])
        part += jnp.dot(tag_err[rows, :], w_ref[...], preferred_element_type=F32)
        item_ref[rows, :] = part.astype(BF16)
        leaving.append(
            pltpu.make_async_copy(item_ref.at[rows], item_hbm.at[rows], out_sems.at[i // step])
        )
        leaving[-1].start()
    half = own_ref.shape[0]
    core = core_ref[0]
    mine, other = (pl.ds(pl.multiple_of(h * half, half), half) for h in (core, 1 - core))
    own_ref[...] = dot_cols(tag_err[:, mine], v_ref[...])
    part = dot_cols(tag_err[:, other], v_ref[...])
    send_ref[...] = part.astype(BF16)
    for copy in leaving:
        copy.wait()


def users_kernel(err_ref, u_ref, v_ref, out_ref):
    step = 256
    for i in range(0, out_ref.shape[0], step):
        rows = pl.ds(i, step)
        grad = jnp.dot(err_ref[rows, :], v_ref[...], preferred_element_type=F32)
        old = u_ref[rows, :].astype(F32)
        out_ref[rows, :] = (old - 0.04 * (grad + 0.05 * old)).astype(BF16)


def split_kernel(bit_ref, own_ref, arrived_ref, keep_ref, send_ref):
    size = keep_ref.shape[0]
    mine, other = (
        pl.ds(pl.multiple_of(h * size, size), size) for h in (bit_ref[0], 1 - bit_ref[0])
    )
    keep_ref[...] = own_ref[mine, :] + arrived_ref[mine, :].astype(F32)
    send_ref[...] = (own_ref[other, :] + arrived_ref[other, :].astype(F32)).astype(BF16)


def item_kernel(tag_ref, v_hbm, pieces_hbm, out_ref, old_ref, pieces_ref, sems):
    count, size = pieces_ref.shape[:2]
    group = count // 4
    start = pl.multiple_of(tag_ref[0] * size, size)
    copies = [
        pltpu.make_async_copy(
            pieces_hbm.at[pl.ds(g * group, group)], pieces_ref.at[pl.ds(g * group, group)], sems.at[g]
        )
        for g in range(4)
    ]
    copies.append(pltpu.make_async_copy(v_hbm.at[pl.ds(start, size)], old_ref, sems.at[4]))
    for copy in copies:
        copy.start()
    total = jnp.zeros(out_ref.shape, F32)
    for g in range(4):
        copies[g].wait()
        for k in range(g * group, (g + 1) * group):
            total += pieces_ref[k].astype(F32)
    copies[4].wait()
    old = old_ref[...].astype(F32)
    out_ref[...] = (old - 0.04 * (total + 0.05 * old)).astype(BF16)


def spread_kernel(shard_ref, out_hbm, sems):
    copies = [
        pltpu.make_async_copy(shard_ref, out_hbm.at[k], sems.at[k])
        for k in range(out_hbm.shape[0])
    ]
    for copy in copies:
        copy.start()
    for copy in copies:
        copy.wait()


def place_kernel(in_ref, out_ref, sems):
    copies = [
        pltpu.make_async_copy(in_ref.at[k], out_ref.at[k], sems.at[k])
        for k in range(out_ref.shape[0])
    ]
    for copy in copies:
        copy.start()
    for copy in copies:
        copy.wait()


def join_kernel(bit_ref, mine_ref, other_ref, out_hbm, sems):
    size = mine_ref.shape[0]
    copies = []
    for k, (ref, index) in enumerate([(mine_ref, bit_ref[0]), (other_ref, 1 - bit_ref[0])]):
        rows = pl.ds(pl.multiple_of(index * size, size), size)
        copies.append(pltpu.make_async_copy(ref, out_hbm.at[rows], sems.at[k]))
        copies[-1].start()
    for copy in copies:
        copy.wait()


def whole():
    return pl.BlockSpec(memory_space=pltpu.VMEM)


def scalars():
    return pl.BlockSpec(memory_space=pltpu.SMEM)


def in_hbm():
    return pl.BlockSpec(memory_space=pltpu.HBM)


def partials(rt, rc, xt, core, u, v, w, r, x):
    users, rank = u.shape
    items, tags = v.shape[0], w.shape[0]
    return pl.pallas_call(
        grads_kernel,
        out_shape=(
            jax.ShapeDtypeStruct((items, rank), BF16),
            jax.ShapeDtypeStruct((tags // 2, rank), BF16),
            jax.ShapeDtypeStruct((tags // 2, rank), F32),
            jax.ShapeDtypeStruct((users, items), BF16),
        ),
        in_specs=[scalars()] * 2 + [in_hbm()] * 7,
        out_specs=(in_hbm(),) + (whole(),) * 3,
        scratch_shapes=[pltpu.SMEM(a.shape, a.dtype) for a in (xt, rt)]
        + [pltpu.VMEM(a.shape, BF16) for a in (u, v, w, r, x)]
        + [
            pltpu.VMEM((items, tags), BF16),
            pltpu.VMEM((items, rank), BF16),
            pltpu.SemaphoreType.DMA((7,)),
            pltpu.SemaphoreType.DMA((items // 256,)),
        ],
        compiler_params=pltpu.CompilerParams(vmem_limit_bytes=14 << 20),
        cost_estimate=pl.CostEstimate(flops=3 << 30, bytes_accessed=6 << 20, transcendentals=0),
    )(rc, core, *(pltpu.with_memory_space_constraint(a, pltpu.HBM) for a in (xt, rt, u, v, w, r, x)))


def updated_users(err, u, v):
    return pl.pallas_call(
        users_kernel,
        out_shape=jax.ShapeDtypeStruct(u.shape, BF16),
        in_specs=[whole()] * 3,
        out_specs=whole(),
        compiler_params=pltpu.CompilerParams(vmem_limit_bytes=6 << 20),
        cost_estimate=pl.CostEstimate(flops=1 << 30, bytes_accessed=4 << 20, transcendentals=0),
    )(err, u, v)


def split_sum(bit, own, arrived):
    size, rank = own.shape[0] // 2, own.shape[1]
    return pl.pallas_call(
        split_kernel,
        out_shape=(
            jax.ShapeDtypeStruct((size, rank), F32),
            jax.ShapeDtypeStruct((size, rank), BF16),
        ),
        in_specs=[scalars(), whole(), whole()],
        out_specs=(whole(),) * 2,
        compiler_params=pltpu.CompilerParams(vmem_limit_bytes=4 << 20),
        cost_estimate=pl.CostEstimate(flops=1 << 18, bytes_accessed=1 << 20, transcendentals=0),
    )(bit, own, arrived)


def updated_items(tag, v, pieces):
    count, size, rank = pieces.shape
    return pl.pallas_call(
        item_kernel,
        out_shape=jax.ShapeDtypeStruct((size, rank), BF16),
        in_specs=[scalars(), in_hbm(), in_hbm()],
        out_specs=whole(),
        scratch_shapes=[
            pltpu.VMEM((size, rank), BF16),
            pltpu.VMEM(pieces.shape, BF16),
            pltpu.SemaphoreType.DMA((5,)),
        ],
        compiler_params=pltpu.CompilerParams(vmem_limit_bytes=4 << 20),
        cost_estimate=pl.CostEstimate(flops=1 << 19, bytes_accessed=1 << 20, transcendentals=0),
    )(tag, *(pltpu.with_memory_space_constraint(a, pltpu.HBM) for a in (v, pieces)))


def spread(shard, count):
    return pl.pallas_call(
        spread_kernel,
        out_shape=jax.ShapeDtypeStruct((count,) + shard.shape, BF16),
        in_specs=[whole()],
        out_specs=in_hbm(),
        scratch_shapes=[pltpu.SemaphoreType.DMA((count,))],
        compiler_params=pltpu.CompilerParams(vmem_limit_bytes=2 << 20),
        cost_estimate=pl.CostEstimate(flops=0, bytes_accessed=1 << 20, transcendentals=0),
    )(shard)


def placed_items(pieces):
    return pl.pallas_call(
        place_kernel,
        out_shape=jax.ShapeDtypeStruct(pieces.shape, BF16),
        in_specs=[pl.BlockSpec(memory_space=pl.ANY)],
        out_specs=in_hbm(),
        scratch_shapes=[pltpu.SemaphoreType.DMA((pieces.shape[0],))],
        compiler_params=pltpu.CompilerParams(vmem_limit_bytes=2 << 20),
        cost_estimate=pl.CostEstimate(flops=0, bytes_accessed=2 << 20, transcendentals=0),
    )(pieces)


def placed_halves(bit, mine, other):
    size, rank = mine.shape
    return pl.pallas_call(
        join_kernel,
        out_shape=jax.ShapeDtypeStruct((2 * size, rank), BF16),
        in_specs=[scalars(), whole(), whole()],
        out_specs=in_hbm(),
        scratch_shapes=[pltpu.SemaphoreType.DMA((2,))],
        compiler_params=pltpu.CompilerParams(vmem_limit_bytes=2 << 20),
        cost_estimate=pl.CostEstimate(flops=0, bytes_accessed=1 << 20, transcendentals=0),
    )(bit, mine, other)


def exchanged(pieces, axis):
    return lax.all_to_all(pieces, axis, 0, 0)


def updated(old, total):
    old = old.astype(F32)
    return (old - 0.04 * (total + 0.05 * old)).astype(BF16)


def part_of(block, index, size):
    return lax.dynamic_slice_in_dim(block, index * size, size, 0)


def swapped(block, mask):
    n = lax.axis_size("rot")
    return lax.ppermute(block, "rot", [(i, i ^ mask) for i in range(n)])


def joined(mine, other, bit):
    return jnp.where(
        bit == 0, jnp.concatenate([mine, other], 0), jnp.concatenate([other, mine], 0)
    )


def added(own, mask):
    own = lax.reduce_precision(own, 8, 7)
    return own + swapped(own.astype(BF16), mask).astype(F32)


def tag_sum_nearby(send, own, y_bit):
    own, send = split_sum(y_bit[None], own, swapped(send, 1))
    return added(own + swapped(send, 4).astype(F32), 8)


def new_tag_rows(total, w, core, y_bit):
    shard = updated(part_of(w, core * 2 + y_bit, total.shape[0]), total)
    half = joined(shard, swapped(shard, 4), y_bit)
    return placed_halves(core[None], half, swapped(half, 1))


def on_device(u, v, w, rating_tiles, rating_counts, ratings, tag_tiles, tag_values):
    rank = u.shape[1]
    n_rot, n_tag = lax.axis_size("rot"), lax.axis_size("tag")
    rot = lax.axis_index("rot")
    core, y_bit = rot & 1, (rot >> 2) & 1
    item_part, tag_send, tag_own, err = partials(
        rating_tiles.T, rating_counts, tag_tiles.T, core[None], u, v, w, ratings, tag_values
    )
    item_pieces = exchanged(item_part.reshape(n_tag, -1, rank), "tag")
    new_users = updated_users(err, u, v)
    tag_total = tag_sum_nearby(tag_send, tag_own, y_bit)
    item_pieces, _, _ = lax.optimization_barrier((item_pieces, tag_total, new_users))
    shard = updated_items(lax.axis_index("tag")[None], v, item_pieces)
    shard = lax.ppermute(shard, "rot", [(i, (i + 1) % n_rot) for i in range(n_rot)])
    tag_total = added(tag_total, 2)
    shard, _ = lax.optimization_barrier((shard, tag_total))
    rotated_items = placed_items(exchanged(spread(shard, n_tag), "tag")).reshape(v.shape)
    new_tags = new_tag_rows(added(tag_total, 16), w, core, y_bit)
    return (new_users, rotated_items, new_tags)


def solution(mesh):
    placed = (
        P(("rot", "tag"), None),
        P("rot", None),
        P("tag", None),
        P(("rot", "tag"), None),
        P(("rot", "tag")),
        P(("rot", "tag"), None, None),
        P(("rot", "tag"), None),
        P(("rot", "tag"), None, None),
    )
    return jax.shard_map(
        on_device,
        mesh=mesh,
        in_specs=placed,
        out_specs=(P(("rot", "tag"), None), P("rot", None), P("tag", None)),
        check_vma=False,
    )
```
